32 devices in a mesh: cons: 4 (over y, core), prod: 8 (over z, x).
Axes of the slice: x: 2, y: 2, z: 4, core: 2. Of those that a mesh axis runs over, the one named last changes fastest.
Arguments:
- tastes: bfloat16 [16384, 128], P('cons'), may hold values from -128 to 128
- price_coef: float32 [16384], P('cons'), may hold values from 0.5 to 5
- characteristics: bfloat16 [16384, 128], P('prod'), may hold values from -6 to 6
- mean_utility: float32 [16384], P('prod'), may hold values from -4 to 4
- panel_cols: int32 [256], replicated, may hold values from 0 to 16383
- firm_map: int32 [16384], P('prod'), may hold values from 0 to 16383, as said below
- inverses: float32 [128, 128, 128], P('prod'), may hold values from -0.5 to 0.5
Outputs:
- shares: float32 [16384], P('prod')
- markup: float32 [16384], P('prod')
- response: float32 [16384, 256], P('prod')
The draws below stay inside these ranges and needn't reach their ends.
Inputs may be any that keep to these rules, and one draw needn't show every extreme that they name: `firm_map`: a permutation of the products; the rows of firm order held by each index of prod name exactly 256 products held by each index of prod.
All inputs are finite; a program needn't handle non-finite values.
Results may differ from the reference program's by a relative error of at most 0.002.
The reference program's roundings to bfloat16 on the way count: a program that leaves them out, or rounds other values in their place, can miss the bound.
Values may be sent and summed in bfloat16 or wider, within the bound.
A program may use at most 64 MiB of HBM per device.

```python
import math
import jax
import jax.numpy as jnp
from jax import lax

K = 128
COLS = 256
B = 128
JD = 2048
J = 16384
I = 16384
F = 128


def drawn_draws(key):
    key_chars, key_tastes = jax.random.split(jax.random.fold_in(key, 7), 2)
    chars_all = jnp.clip(jax.random.normal(key_chars, (J, K), jnp.float32), -6.0, 6.0)
    tastes_all = jnp.clip(jax.random.normal(key_tastes, (I, K), jnp.float32), -6.0, 6.0) * (3.0 / math.sqrt(K))
    return (chars_all, tastes_all)


def draw_characteristics(key, part):
    return drawn_draws(key)[0].astype(jnp.bfloat16)


def draw_tastes(key, part):
    return drawn_draws(key)[1].astype(jnp.bfloat16)


def shuffle_one(subkey):
    return jax.random.permutation(subkey, JD).astype(jnp.int32)


def draw_firm_map(key, part):
    sources = J // JD
    per_pair = JD // sources
    key_first, key_second = jax.random.split(jax.random.fold_in(key, 11))
    shuffled = jax.vmap(shuffle_one)(jax.random.split(key_first, sources))
    owned = shuffled + (jnp.arange(sources, dtype=jnp.int32) * JD)[:, None]
    routed = owned.reshape(sources, sources, per_pair).transpose(1, 0, 2).reshape(sources, JD)
    mixing = jax.vmap(shuffle_one)(jax.random.split(key_second, sources))
    mixed = jnp.take_along_axis(routed, mixing, axis=1)
    return mixed.reshape(J).astype(jnp.int32)


def with_ends(result, rng, smallest, top_value):
    longest = result.shape.index(max(result.shape))
    spots = []
    for shift in (0, 1):
        where = [jax.random.randint(jax.random.fold_in(rng, axis), (), 0, length) for axis, length in enumerate(result.shape)]
        where[longest] = (where[longest] + shift) % result.shape[longest]
        spots.append(tuple(where))
    return result.at[spots[0]].set(smallest).at[spots[1]].set(top_value)


def block_scale(own_key, extent, shards, least, largest):
    gain = 1.0
    for position, shards_of in shards:
        steps = jax.random.uniform(jax.random.fold_in(jax.random.fold_in(own_key, 6), position), (shards_of,), jnp.float32, least / len(shards), largest / len(shards))
        gain = gain * jnp.repeat(jnp.exp(steps), extent[position] // shards_of).reshape((-1,) + (1,) * (len(extent) - 1 - position))
    return gain


def gaussian(stream_key, shape, scale, most, cuts=(), held_as=jnp.bfloat16):
    drawn = scale * jax.random.normal(stream_key, shape, jnp.float32)
    if cuts:
        drawn = drawn * block_scale(stream_key, shape, cuts, -0.22, 0.18)
    return jnp.clip(drawn, -most, most).astype(held_as)


def setup_inputs(seed: int = 0) -> dict:
    streams_of = jax.random.split(jax.random.key(seed), 8)
    return {
        "tastes": draw_tastes(jax.random.fold_in(streams_of[7], 71), 0),
        "price_coef": jnp.clip(jnp.exp(math.log(5.0) - 2.3025851 * jax.random.uniform(streams_of[1], (I,), jnp.float32) ** block_scale(streams_of[1], (I,), ((0, 4),), -0.2, 0.2)), 0.5, 5.0),
        "characteristics": draw_characteristics(jax.random.fold_in(streams_of[7], 71), 0),
        "mean_utility": gaussian(streams_of[3], (J,), 1.0, 4.0, ((0, 8),), jnp.float32),
        "panel_cols": with_ends(jax.random.randint(streams_of[4], (COLS,), 0, J), jax.random.fold_in(streams_of[4], 1), 0, J - 1).astype(jnp.int32),
        "firm_map": draw_firm_map(jax.random.fold_in(streams_of[7], 71), 0),
        "inverses": gaussian(streams_of[6], (F, B, B), B ** -0.5, 0.5, ((0, 8),), jnp.float32),
    }


def reference(tastes, price_coef, characteristics, mean_utility, panel_cols, firm_map, inverses):
    count_products = characteristics.shape[0]
    count_consumers = tastes.shape[0]
    block_rows = min(512, count_consumers)
    block_count = count_consumers // block_rows
    col_chars = characteristics[panel_cols]
    col_means = mean_utility[panel_cols]
    taste_blocks = tastes.reshape(block_count, block_rows, tastes.shape[1])
    coef_blocks = price_coef.reshape(block_count, block_rows)

    def consume(state_now, inputs):
        panel_sum, share_sum, diag_sum = state_now
        taste_block, coef_block = inputs
        utility = jnp.dot(taste_block, characteristics.T, preferred_element_type=jnp.float32) + mean_utility[None, :]
        highest = jnp.maximum(jnp.max(utility, axis=1), 0.0)
        exponent = jnp.exp(utility - highest[:, None])
        denominator = jnp.exp(-highest) + jnp.sum(exponent, axis=1)
        scaled = count_products * exponent / denominator[:, None]
        share_sum = share_sum + jnp.sum(scaled, axis=0)
        diag_sum = diag_sum + jnp.dot(coef_block, scaled, precision=lax.Precision.HIGHEST)
        col_util = jnp.dot(taste_block, col_chars.T, preferred_element_type=jnp.float32) + col_means[None, :]
        col_scaled = count_products * jnp.exp(col_util - highest[:, None]) / denominator[:, None]
        weighted = (coef_block[:, None] * col_scaled).astype(jnp.bfloat16)
        panel_sum = panel_sum + lax.dot_general(scaled.astype(jnp.bfloat16), weighted, (((0,), (0,)), ((), ())), preferred_element_type=jnp.float32)
        return (panel_sum, share_sum, diag_sum), None

    start_state = (jnp.zeros((count_products, panel_cols.shape[0]), jnp.float32), jnp.zeros((count_products,), jnp.float32), jnp.zeros((count_products,), jnp.float32))
    (panel_sum, share_sum, diag_sum), _ = lax.scan(consume, start_state, (taste_blocks, coef_blocks))
    cross = panel_sum / count_consumers
    shares = share_sum / count_consumers
    diagonal = diag_sum / count_consumers
    product_ids = jnp.arange(count_products, dtype=jnp.int32)
    marks = (product_ids[:, None] == panel_cols[None, :]).astype(jnp.float32)
    jacobian = cross - diagonal[:, None] * marks
    block_size = inverses.shape[1]
    firm_count = inverses.shape[0]
    ordered = jacobian[firm_map].reshape(firm_count, block_size, panel_cols.shape[0])
    response = jnp.einsum("fab,fbc->fac", inverses, ordered, precision=lax.Precision.HIGHEST).reshape(count_products, panel_cols.shape[0])
    ordered_shares = shares[firm_map].reshape(firm_count, block_size)
    markup = jnp.einsum("fab,fb->fa", inverses, ordered_shares, precision=lax.Precision.HIGHEST).reshape(count_products)
    return shares, markup, response
```

```python
import functools
import jax
import jax.numpy as jnp
from jax import lax
from jax.experimental import pallas as pl
from jax.experimental.pallas import tpu as pltpu
from jax.sharding import PartitionSpec as P

F32 = jnp.float32
BF16 = jnp.bfloat16
NT = (((1,), (1,)), ((), ()))
MESH = pl.DeviceIdType.MESH
VMEM = pl.BlockSpec(memory_space=pltpu.VMEM)
LIMIT = 63 * 1024 * 1024


def lanes(count):
    return -(-count // 128) * 128


def turned(row):
    return jnp.broadcast_to(row, (128, 128)).T


def thirds(x):
    a = x.astype(BF16).astype(F32)
    b = (x - a).astype(BF16).astype(F32)
    return a, b, x - a - b


def split(column, width):
    lane = lax.broadcasted_iota(jnp.int32, (column.shape[0], width), 1)
    a, b, c = thirds(column)
    return jnp.where(lane == 0, a, jnp.where(lane == 1, b, jnp.where(lane == 2, c, 0.0))).astype(BF16)


def rows_of(shape):
    return lax.broadcasted_iota(jnp.int32, shape, 0).astype(F32)


def step_kernel(
    n, cp, room, pad, count_products, count_consumers, IC, WC, JT, GR,
    fm, cols, chars, mean, tastes, coef, inv,
    out, mk, home,
    CA, TA, CF, TB, MS2, KEY, BT, sid, asked,
    X, XM, R, RM, XC, XCM, RC, RCM, CP, CC,
    UA, MS, PK, FV, WT,
    UB, SCB, SH, DG, PO, PX, PR, YS, YR, ST, SV, HV,
    a_s, a_r, x_s, x_r, f_s, f_r, m_s, m_r, c_s, c_r, k_s, k_r, cc_s, cc_r,
    ms_s, ms_r, px_s, px_r, y_s, y_r, o_s, o_r, st_s, st_r, h_s, h_r,
):
    me = lax.axis_index("prod")
    cons = lax.axis_index("cons")
    core = lax.rem(cons, 2)
    partner = cons + 1 - 2 * core
    across = lax.rem(cons + 2, 4)
    LP, K = chars.shape
    LI = tastes.shape[0]
    W = cols.shape[1]
    half = W // 2
    block = inv.shape[1]
    pp = LP // n
    nb, pb = LP // 128, pad // 128
    nc, nw, nt = LI // IC, LI // WC, LP // JT
    base = me * LP

    barrier = pltpu.get_barrier_semaphore()
    for d in range(1, n):
        pl.semaphore_signal(barrier, inc=1, device_id={"prod": lax.rem(me + d, n)}, device_id_type=MESH)
    for d in range(1, 4):
        pl.semaphore_signal(barrier, inc=1, device_id={"cons": lax.rem(cons + d, 4)}, device_id_type=MESH)

    def loop(fn, lo=1):
        def step(d, carry):
            fn(d)
            return carry
        lax.fori_loop(lo, n, step, 0)

    def to_prod(src, dst, s, r, d):
        return pltpu.make_async_remote_copy(
            src, dst, s.at[d], r.at[d],
            device_id={"prod": lax.rem(me + d, n)}, device_id_type=MESH,
        )

    def to_cons(src, dst, s, r, peer):
        return pltpu.make_async_remote_copy(src, dst, s, r, device_id={"cons": peer}, device_id_type=MESH)

    fmf = fm[...].astype(F32)
    source = jnp.floor((fmf + 0.5) * (1.0 / LP))
    local = fmf - source * float(LP)
    owners = rows_of((n, 128))
    marks = jnp.concatenate(
        [jnp.where(source[:, b * 128:(b + 1) * 128] == owners, 1.0, 0.0) for b in range(nb)], axis=0
    )
    at0 = lax.broadcasted_iota(jnp.int32, (128, 128), 0)
    at1 = lax.broadcasted_iota(jnp.int32, (128, 128), 1)
    before = jnp.where(at0 < at1, 1.0, 0.0).astype(BF16)
    inner = jnp.dot(marks.astype(BF16), before, preferred_element_type=F32)
    totals = jnp.dot(marks.astype(BF16), jnp.ones((128, 128), BF16), preferred_element_type=F32)
    q0 = lax.broadcasted_iota(jnp.int32, (nb * n, nb * n), 0).astype(F32)
    q1 = lax.broadcasted_iota(jnp.int32, (nb * n, nb * n), 1).astype(F32)
    b0, b1 = jnp.floor((q0 + 0.5) * (1.0 / n)), jnp.floor((q1 + 0.5) * (1.0 / n))
    earlier = jnp.where((q0 - b0 * n == q1 - b1 * n) & (b1 < b0), 1.0, 0.0).astype(BF16)
    offset = jnp.dot(earlier, totals.astype(BF16), preferred_element_type=F32)
    placed = marks * (inner + offset)
    slot = jnp.concatenate(
        [jnp.sum(placed[b * n:(b + 1) * n], axis=0, keepdims=True) for b in range(nb)], axis=1
    )
    high = jnp.floor((slot + 0.5) * (1.0 / 128))
    KEY[...] = source * float(pb) + high
    BT[...] = jnp.where(slot - high * 128.0 == rows_of((128, LP)), 1.0, 0.0).astype(BF16)

    def scatter(parts):
        mask = KEY[...] == rows_of((n * pb, LP))
        left = jnp.concatenate([jnp.where(mask, p, 0.0) for p in parts], axis=0).astype(BF16)
        got = lax.dot_general(left, BT[...], NT, preferred_element_type=F32)
        return [got[k * n * pb:(k + 1) * n * pb] for k in range(len(parts))]

    upper = jnp.floor((local + 0.5) * (1.0 / 128))
    hi, lo = scatter([upper, local - upper * 128.0])
    q = rows_of((n * pb, 128))
    owner = jnp.floor((q + 0.5) * (1.0 / pb))
    place = (q - owner * pb) * 128.0 + lax.broadcasted_iota(jnp.int32, (n * pb, 128), 1).astype(F32)
    wanted = jnp.where(place < float(pp), owner * float(LP) + hi * 128.0 + lo, -1.0).astype(jnp.int32)
    for p in range(n):
        for b in range(pb):
            sid[p, :, b * 128:(b + 1) * 128] = wanted[p * pb + b:p * pb + b + 1]

    CA[:, :K] = chars[...]

    def widen(g, carry):
        rows = pl.ds(pl.multiple_of(g * 128, 128), 128)
        CA[rows, K:] = split(turned(mean[:, rows]), K)
        return carry

    lax.fori_loop(0, nb, widen, 0)
    TA[:, :K] = tastes[...]
    TA[:, K:] = jnp.where(lax.broadcasted_iota(jnp.int32, (LI, K), 1) < 3, 1.0, 0.0).astype(BF16)
    pl.semaphore_wait(barrier, n + 2)

    def a_copy(d):
        return to_prod(sid.at[lax.rem(me + d, n)], asked.at[me], a_s, a_r, d)

    loop(lambda d: a_copy(d).start())
    asked[me] = sid[me]

    def pick(wants):
        spot = lax.broadcasted_iota(jnp.int32, (128, 128), 1).astype(F32)
        bands = []
        for w in wants:
            want = turned((w - base).astype(F32))
            bands.append(jnp.concatenate(
                [jnp.where(want == spot + float(b * 128), 1.0, 0.0).astype(BF16) for b in range(nb)], axis=1
            ))
        got = jnp.dot(jnp.concatenate(bands, axis=0), CA[...], preferred_element_type=F32)
        means = []
        for k in range(len(wants)):
            t = got[k * 128:(k + 1) * 128, K:].T
            means.append(t[0:1] + (t[1:2] + t[2:3]))
        return got[:, :K].astype(BF16), means

    rows, means = pick([cols[:, g * 128:(g + 1) * 128] for g in range(W // 128)])
    XC[:, :cp, :] = rows.astype(F32).reshape(n, cp, K).astype(BF16)
    for g in range(W // 128):
        XCM[:, g * 128:(g + 1) * 128] = means[g]

    def c_copy(d):
        return to_prod(XC.at[lax.rem(me + d, n)], RC.at[me], c_s, c_r, d)

    def k_copy(d):
        return to_prod(XCM, RCM.at[me], k_s, k_r, d)

    loop(lambda d: c_copy(d).start())
    loop(lambda d: k_copy(d).start())
    RC[me] = XC[me]
    RCM[me] = XCM[...]

    def ms_copy(d, ic):
        return to_prod(MS.at[0, ic], MS.at[d, ic], ms_s.at[ic], ms_r.at[ic], d)

    def stats(ic, carry):
        i0 = pl.multiple_of(ic * IC, IC)
        u = lax.dot_general(CA[...], TA[pl.ds(i0, IC), :], NT, preferred_element_type=F32)
        UA[...] = u
        m = jnp.maximum(jnp.max(u, axis=0, keepdims=True), 0.0)
        s8 = jnp.sum(jnp.exp(UA[...] - m).reshape(LP // 8, 8, IC), axis=0)
        MS[0, ic, 0:1, :] = m
        MS[0, ic, 1:2, :] = jnp.sum(s8, axis=0, keepdims=True)
        loop(lambda d: ms_copy(d, ic).start())
        return carry

    def cc_copy(d):
        return to_prod(CP, CC.at[me], cc_s, cc_r, d)

    span = pad // 2
    part = pl.ds(pl.multiple_of(core * span, span), span)

    def x_copy(d):
        return to_prod(X.at[lax.rem(me + d, n), part], R.at[me, part], x_s, x_r, d)

    def m_copy(d):
        return to_prod(XM.at[lax.rem(me + d, n)], RM.at[me], m_s, m_r, d)

    def f_copy(d):
        src = lax.rem(me + n - d, n)
        return to_cons(R.at[src, part], R.at[src, part], f_s.at[d], f_r.at[d], partner)

    lax.fori_loop(0, nc // 2, stats, 0)
    loop(lambda d: c_copy(d).wait())
    loop(lambda d: k_copy(d).wait())
    total = RC[0, :cp, :].astype(F32)
    heads = RCM[0]
    for p in range(1, n):
        total = total + RC[p, :cp, :].astype(F32)
        heads = heads + RCM[p]
    CP[...] = total
    loop(lambda d: cc_copy(d).start())
    CC[me] = CP[...]

    def answer(d, carry):
        src = lax.rem(me + n - d, n)

        @pl.when(d > 0)
        def _():
            a_copy(lax.rem(n - d, n)).wait_send()
            a_copy(d).wait_recv()

        rows, means = pick([asked[src, :, b * 128:(b + 1) * 128] for b in range(pb)])
        X[src] = rows
        for b in range(pb):
            XM[src, :, b * 128:(b + 1) * 128] = means[b]

        @pl.when(d > 0)
        def _():
            back = lax.rem(n - d, n)
            x_copy(back).start()
            m_copy(back).start()

        return carry

    lax.fori_loop(0, n, answer, 0)
    R[me] = X[me]
    RM[me] = XM[me]
    lax.fori_loop(nc // 2, nc, stats, 0)

    def relay(d):
        x_copy(d).wait()
        f_copy(d).start()

    loop(relay)

    loop(lambda d: cc_copy(d).wait())
    ccv = CC[...].reshape(n * cp, K).astype(BF16)
    cm = jnp.concatenate([turned(heads[:, g * 128:(g + 1) * 128])[:, :1] for g in range(W // 128)], axis=0)

    def weights(ic):
        loop(lambda d: ms_copy(d, ic).wait())
        for w in range(IC // WC):
            i0 = pl.multiple_of(ic * IC + w * WC, WC)
            at = slice(w * WC, (w + 1) * WC)
            peak = MS[0, ic, 0:1, at]
            for d in range(1, n):
                peak = jnp.maximum(peak, MS[d, ic, 0:1, at])
            den = jnp.exp(-peak)
            for d in range(n):
                den = den + MS[d, ic, 1:2, at] * jnp.exp(MS[d, ic, 0:1, at] - peak)
            f = count_products / den
            PK[:, pl.ds(i0, WC)] = peak
            FV[:, pl.ds(i0, WC)] = f
            cu = lax.dot_general(ccv, tastes[pl.ds(i0, WC), :], NT, preferred_element_type=F32) + cm
            w = coef[:, pl.ds(i0, WC)] * (f * jnp.exp(cu - peak))
            WT[pl.ds(i0, WC), :] = w.T.astype(BF16)

    def weights_step(ic, carry):
        weights(ic)
        return carry

    lax.fori_loop(0, nc, weights_step, 0)

    loop(lambda d: m_copy(d).wait())
    loop(lambda d: f_copy(d).wait())

    def table(p, carry):
        at = pl.ds(pl.multiple_of(p * pad, pad), pad)
        TB[at, :K] = R[p]
        TB[at, K:] = jnp.concatenate(
            [split(turned(RM[p, :, b * 128:(b + 1) * 128]), K) for b in range(pb)], axis=0
        )
        return carry

    lax.fori_loop(0, n, table, 0)

    def firm(g, carry):
        bands = []
        for h in range(4):
            rows = pl.ds(pl.multiple_of(g * 512 + h * 128, 128), 128)
            want = turned(fm[:, rows].astype(F32))
            bands.append(jnp.concatenate(
                [
                    jnp.where(want == sid[p, :, b * 128:(b + 1) * 128].astype(F32), 1.0, 0.0).astype(BF16)
                    for p in range(n) for b in range(pb)
                ],
                axis=1,
            ))
        rows = pl.ds(pl.multiple_of(g * 512, 512), 512)
        CF[rows, :] = jnp.dot(jnp.concatenate(bands, axis=0), TB[...], preferred_element_type=F32).astype(BF16)
        return carry

    lax.fori_loop(0, LP // 512, firm, 0)

    def halves(fb, carry):
        m = inv[fb]
        h = m.astype(BF16)
        MS2[fb, :, :block] = h
        MS2[fb, :, block:] = (m - h.astype(F32)).astype(BF16)
        return carry

    lax.fori_loop(0, LP // block, halves, 0)

    def tile_rows(jt):
        return pl.ds(pl.multiple_of(jt * JT, JT), JT)

    def px_copy(jt):
        rows = tile_rows(jt)
        return to_cons(PX.at[rows], PR.at[rows], px_s.at[jt], px_r.at[jt], partner)

    def y_copy(jt):
        rows = tile_rows(jt)
        return to_cons(YS.at[rows], YR.at[rows], y_s.at[jt], y_r.at[jt], across)

    mine = pl.ds(pl.multiple_of(core * half, half), half)

    def o_copy(jt):
        rows = tile_rows(jt)
        return to_cons(out.at[rows, mine], out.at[rows, mine], o_s.at[jt], o_r.at[jt], partner)

    def st_copy(d):
        return to_cons(ST.at[cons], ST.at[cons], st_s.at[d], st_r.at[d], lax.rem(cons + d, 4))

    def forward(jt):
        rows = tile_rows(jt)
        px_copy(jt).wait()
        YS[rows, :] = (PO[rows, :] + PR[rows, :]).astype(BF16)
        y_copy(jt).start()

    def finish(jt):
        y_copy(jt).wait()
        for b in range(JT // block):
            rows = pl.ds(pl.multiple_of(jt * JT + b * block, block), block)
            x = (YS[rows, :].astype(F32) + YR[rows, :].astype(F32)) / count_consumers
            h = x.astype(BF16)
            pair = jnp.concatenate([h, (x - h.astype(F32)).astype(BF16)], axis=1)
            both = jnp.concatenate([pair, pair], axis=0)
            r = jnp.dot(MS2[jt * (JT // block) + b], both, preferred_element_type=F32)
            out[rows, mine] = r[:, :half] + r[:, half:]
        o_copy(jt).start()

    heads_row = cols[...].astype(F32)

    def panel(jt, carry):
        rows = tile_rows(jt)
        UB[...] = lax.dot_general(CF[rows, :], TA[...], NT, preferred_element_type=F32)
        for g in range(JT // GR):
            band = pl.ds(g * GR, GR)
            sh = jnp.zeros((GR, 128), F32)
            dg = jnp.zeros((GR, 128), F32)
            for b in range(LI // 128):
                at = pl.ds(b * 128, 128)
                sc = jnp.exp(UB[band, at] - PK[:, at]) * FV[:, at]
                SCB[band, at] = sc.astype(BF16)
                sh = sh + sc
                dg = dg + sc * coef[:, at]
            SH[band, :] = sh
            DG[band, :] = dg
        acc = jnp.dot(SCB[...], WT[...], preferred_element_type=F32)
        ST[cons, 0:1, rows] = jnp.sum(SH[...].T, axis=0, keepdims=True)
        diag = jnp.sum(DG[...], axis=1, keepdims=True)
        ids = jnp.concatenate(
            [
                turned(fm[:, pl.ds(pl.multiple_of(jt * JT + b * 128, 128), 128)].astype(F32))[:, :1]
                for b in range(JT // 128)
            ],
            axis=0,
        )
        acc = acc - jnp.where(ids == heads_row, diag, 0.0)
        first, second = acc[:, :half], acc[:, half:]
        PO[rows, :] = jnp.where(core == 0, first, second)
        PX[rows, :] = jnp.where(core == 0, second, first)
        px_copy(jt).start()

        @pl.when(jt > 0)
        def _():
            forward(jt - 1)

        @pl.when(jt > 1)
        def _():
            finish(jt - 2)

        return carry

    lax.fori_loop(0, nt, panel, 0)
    for d in range(1, 4):
        st_copy(d).start()
    forward(nt - 1)
    for d in range(1, 4):
        st_copy(d).wait()
    share = (ST[0] + ST[1] + ST[2] + ST[3]) / count_consumers
    sums = scatter(thirds(share))
    slots = sums[0] + (sums[1] + sums[2])
    for p in range(n):
        for b in range(pb):
            SV[p, :, b * 128:(b + 1) * 128] = slots[p * pb + b:p * pb + b + 1]

    def h_copy(d):
        return to_prod(SV.at[lax.rem(me + d, n)], HV.at[me], h_s, h_r, d)

    loop(lambda d: h_copy(d).start())
    HV[me] = SV[me]
    for t in range(max(nt - 2, 0), nt - 1):
        finish(t)
    s1 = share.astype(BF16)
    s2 = (share - s1.astype(F32)).astype(BF16)
    for fb in range(LP // block):
        at = slice(fb * block, (fb + 1) * block)
        pair = jnp.concatenate([s1[:, at], s1[:, at]], axis=1).astype(F32)
        rest = jnp.concatenate([s2[:, at], s2[:, at]], axis=1).astype(F32)
        left = jnp.concatenate([jnp.broadcast_to(pair, (8, 2 * block)), jnp.broadcast_to(rest, (8, 2 * block))], axis=0)
        r = lax.dot_general(left.astype(BF16), MS2[fb], NT, preferred_element_type=F32)
        mk[fb:fb + 1, :] = r[0:1] + r[8:9]
    finish(nt - 1)

    loop(lambda d: h_copy(d).wait())
    ids = jnp.concatenate([asked[p] for p in range(n)], axis=1) - base
    idf = ids.astype(F32)
    up = jnp.floor((idf + 0.5) * (1.0 / 128))
    right = jnp.where(idf - up * 128.0 == rows_of((128, n * pad)), 1.0, 0.0).astype(BF16)
    mask = up == rows_of((nb, n * pad))
    back = jnp.concatenate([HV[p] for p in range(n)], axis=1)
    left = jnp.concatenate([jnp.where(mask, p, 0.0) for p in thirds(back)], axis=0).astype(BF16)
    got = lax.dot_general(left, right, NT, preferred_element_type=F32)
    home[...] = got[:nb] + (got[nb:2 * nb] + got[2 * nb:])

    def drain(jt, carry):
        o_copy(jt).wait()
        return carry

    lax.fori_loop(0, nt, drain, 0)


def run(n, count_products, count_consumers, fm, cols, chars, mean, tastes, coef, inv):
    LP, K = chars.shape
    LI, W = tastes.shape[0], cols.shape[1]
    block = inv.shape[1]
    half = W // 2
    cp = W // n
    room = -(-cp // 16) * 16
    pad = lanes(LP // n)
    IC, WC, JT, GR = min(1024, LI), min(512, LI), min(512, LP), 32
    nc, nt = LI // IC, LP // JT
    nb, pb = LP // 128, pad // 128
    dma = pltpu.SemaphoreType.DMA
    vm = pltpu.VMEM
    I32 = jnp.int32
    return pl.pallas_call(
        functools.partial(
            step_kernel, n, cp, room, pad, float(count_products), float(count_consumers), IC, WC, JT, GR
        ),
        out_shape=(
            jax.ShapeDtypeStruct((LP, W), F32),
            jax.ShapeDtypeStruct((LP // block, block), F32),
            jax.ShapeDtypeStruct((nb, 128), F32),
        ),
        in_specs=[VMEM] * 7,
        out_specs=(VMEM,) * 3,
        scratch_shapes=[
            vm((LP, 2 * K), BF16), vm((LI, 2 * K), BF16), vm((LP, 2 * K), BF16), vm((n * pad, 2 * K), BF16),
            vm((LP // block, block, 2 * block), BF16), vm((1, LP), F32), vm((128, LP), BF16),
            vm((n, 1, pad), I32), vm((n, 1, pad), I32),
            vm((n, pad, K), BF16), vm((n, 1, pad), F32), vm((n, pad, K), BF16), vm((n, 1, pad), F32),
            vm((n, room, K), BF16), vm((1, W), F32), vm((n, room, K), BF16), vm((n, 1, W), F32),
            vm((cp, K), F32), vm((n, cp, K), F32),
            vm((LP, IC), F32), vm((n, nc, 2, IC), F32), vm((1, LI), F32), vm((1, LI), F32), vm((LI, W), BF16),
            vm((JT, LI), F32), vm((JT, LI), BF16), vm((JT, 128), F32), vm((JT, 128), F32),
            vm((LP, half), F32), vm((LP, half), F32), vm((LP, half), F32),
            vm((LP, half), BF16), vm((LP, half), BF16),
            vm((4, 1, LP), F32), vm((n, 1, pad), F32), vm((n, 1, pad), F32),
        ] + [dma((n,))] * 14 + [dma((nc, n))] * 2 + [dma((nt,))] * 6 + [dma((4,))] * 2 + [dma((n,))] * 2,
        compiler_params=pltpu.CompilerParams(collective_id=1, has_side_effects=True, vmem_limit_bytes=LIMIT),
    )(fm, cols, chars, mean, tastes, coef, inv)


def body(tastes, price_coef, characteristics, mean_utility, panel_cols, firm_map, inverses):
    n = lax.axis_size("prod")
    LP = characteristics.shape[0]
    response, markup, shares = run(
        n, LP * n, tastes.shape[0] * lax.axis_size("cons"),
        firm_map[None, :], panel_cols[None, :], characteristics, mean_utility[None, :],
        tastes, price_coef[None, :], inverses,
    )
    return shares.reshape(LP), markup.reshape(LP), response


def solution(mesh):
    return jax.shard_map(
        body,
        mesh=mesh,
        in_specs=(
            P("cons", None),
            P("cons"),
            P("prod", None),
            P("prod"),
            P(),
            P("prod"),
            P("prod", None, None),
        ),
        out_specs=(P("prod"), P("prod"), P("prod", None)),
        check_vma=False,
    )
```

```python
import functools
import jax
import jax.numpy as jnp
from jax import lax
from jax.experimental import pallas as pl
from jax.experimental.pallas import tpu as pltpu
from jax.sharding import PartitionSpec as P

F32 = jnp.float32
BF16 = jnp.bfloat16
NT = (((1,), (1,)), ((), ()))
MESH = pl.DeviceIdType.MESH
VMEM = pl.BlockSpec(memory_space=pltpu.VMEM)
LIMIT = 63 * 1024 * 1024


def lanes(count):
    return -(-count // 128) * 128


def turned(row):
    return jnp.broadcast_to(row, (128, 128)).T


def thirds(x):
    a = x.astype(BF16).astype(F32)
    b = (x - a).astype(BF16).astype(F32)
    return a, b, x - a - b


def split(column, width):
    lane = lax.broadcasted_iota(jnp.int32, (column.shape[0], width), 1)
    a, b, c = thirds(column)
    return jnp.where(lane == 0, a, jnp.where(lane == 1, b, jnp.where(lane == 2, c, 0.0))).astype(BF16)


def rows_of(shape):
    return lax.broadcasted_iota(jnp.int32, shape, 0).astype(F32)


def step_kernel(
    n, cp, room, pad, count_products, count_consumers, IC, WC, JT, GR,
    fm, cols, chars, mean, tastes, coef,
    out, srow, home,
    CA, TA, CF, TB, KEY, BT, sid, asked,
    X, XM, R, RM, XC, XCM, RC, RCM, CP, CC,
    UA, MS, PK, FV, WT,
    XO, UB, SCB, SH, DG, PO, PX, PR, YS, YR, ST, SV, HV,
    i_s, w_s, a_s, a_r, x_s, x_r, f_s, f_r, m_s, m_r, c_s, c_r, k_s, k_r, cc_s, cc_r,
    ms_s, ms_r, px_s, px_r, y_s, y_r, o_s, o_r, st_s, st_r, h_s, h_r,
):
    me = lax.axis_index("prod")
    cons = lax.axis_index("cons")
    core = lax.rem(cons, 2)
    partner = cons + 1 - 2 * core
    across = lax.rem(cons + 2, 4)
    LP, K = chars.shape
    LI = tastes.shape[0]
    W = cols.shape[1]
    half = W // 2
    pp = LP // n
    nb, pb = LP // 128, pad // 128
    nc, nw, nt = LI // IC, LI // WC, LP // JT
    base = me * LP

    barrier = pltpu.get_barrier_semaphore()
    for d in range(1, n):
        pl.semaphore_signal(barrier, inc=1, device_id={"prod": lax.rem(me + d, n)}, device_id_type=MESH)
    for d in range(1, 4):
        pl.semaphore_signal(barrier, inc=1, device_id={"cons": lax.rem(cons + d, 4)}, device_id_type=MESH)

    def loop(fn, lo=1):
        def step(d, carry):
            fn(d)
            return carry
        lax.fori_loop(lo, n, step, 0)

    def to_prod(src, dst, s, r, d):
        return pltpu.make_async_remote_copy(
            src, dst, s, r,
            device_id={"prod": lax.rem(me + d, n)}, device_id_type=MESH,
        )

    rest = pl.ds(0, n - 1)

    def all_of(ref, s, r):
        return to_prod(ref, ref, s, r, 1)

    def to_cons(src, dst, s, r, peer):
        return pltpu.make_async_remote_copy(src, dst, s, r, device_id={"cons": peer}, device_id_type=MESH)

    load_chars = pltpu.make_async_copy(chars, CA.at[:, pl.ds(0, K)], i_s.at[0])
    load_tastes = pltpu.make_async_copy(tastes, TA.at[:, pl.ds(0, K)], i_s.at[1])
    load_chars.start()
    load_tastes.start()

    fmf = fm[...].astype(F32)
    source = jnp.floor((fmf + 0.5) * (1.0 / LP))
    local = fmf - source * float(LP)
    owners = rows_of((n, 128))
    marks = jnp.concatenate(
        [jnp.where(source[:, b * 128:(b + 1) * 128] == owners, 1.0, 0.0) for b in range(nb)], axis=0
    )
    at0 = lax.broadcasted_iota(jnp.int32, (128, 128), 0)
    at1 = lax.broadcasted_iota(jnp.int32, (128, 128), 1)
    before = jnp.where(at0 < at1, 1.0, 0.0).astype(BF16)
    inner = jnp.dot(marks.astype(BF16), before, preferred_element_type=F32)
    totals = jnp.dot(marks.astype(BF16), jnp.ones((128, 128), BF16), preferred_element_type=F32)
    q0 = lax.broadcasted_iota(jnp.int32, (nb * n, nb * n), 0).astype(F32)
    q1 = lax.broadcasted_iota(jnp.int32, (nb * n, nb * n), 1).astype(F32)
    b0, b1 = jnp.floor((q0 + 0.5) * (1.0 / n)), jnp.floor((q1 + 0.5) * (1.0 / n))
    earlier = jnp.where((q0 - b0 * n == q1 - b1 * n) & (b1 < b0), 1.0, 0.0).astype(BF16)
    offset = jnp.dot(earlier, totals.astype(BF16), preferred_element_type=F32)
    placed = marks * (inner + offset)
    slot = jnp.concatenate(
        [jnp.sum(placed[b * n:(b + 1) * n], axis=0, keepdims=True) for b in range(nb)], axis=1
    )
    high = jnp.floor((slot + 0.5) * (1.0 / 128))
    KEY[...] = source * float(pb) + high
    BT[...] = jnp.where(slot - high * 128.0 == rows_of((128, LP)), 1.0, 0.0).astype(BF16)

    def scatter(parts):
        mask = KEY[...] == rows_of((n * pb, LP))
        left = jnp.concatenate([jnp.where(mask, p, 0.0) for p in parts], axis=0).astype(BF16)
        got = lax.dot_general(left, BT[...], NT, preferred_element_type=F32)
        return [got[k * n * pb:(k + 1) * n * pb] for k in range(len(parts))]

    upper = jnp.floor((local + 0.5) * (1.0 / 128))
    hi, lo = scatter([upper, local - upper * 128.0])
    q = rows_of((n * pb, 128))
    owner = jnp.floor((q + 0.5) * (1.0 / pb))
    place = (q - owner * pb) * 128.0 + lax.broadcasted_iota(jnp.int32, (n * pb, 128), 1).astype(F32)
    wanted = jnp.where(place < float(pp), owner * float(LP) + hi * 128.0 + lo, -1.0).astype(jnp.int32)
    for p in range(n):
        for b in range(pb):
            sid[p, :, b * 128:(b + 1) * 128] = wanted[p * pb + b:p * pb + b + 1]

    pl.semaphore_wait(barrier, n + 2)

    def a_copy(d):
        return to_prod(sid.at[lax.rem(me + d, n)], asked.at[me], a_s.at[0], a_r.at[d], d)

    loop(lambda d: a_copy(d).start())
    asked[me] = sid[me]

    for g in range(nb):
        CA[g * 128:(g + 1) * 128, K:] = split(turned(mean[:, g * 128:(g + 1) * 128]), K)
    TA[:, K:] = jnp.where(lax.broadcasted_iota(jnp.int32, (LI, K), 1) < 3, 1.0, 0.0).astype(BF16)
    load_chars.wait()

    def pick(wants):
        spot = lax.broadcasted_iota(jnp.int32, (128, 128), 1).astype(F32)
        bands = []
        for w in wants:
            want = turned((w - base).astype(F32))
            bands.append(jnp.concatenate(
                [jnp.where(want == spot + float(b * 128), 1.0, 0.0).astype(BF16) for b in range(nb)], axis=1
            ))
        got = jnp.dot(jnp.concatenate(bands, axis=0), CA[...], preferred_element_type=F32)
        means = []
        for k in range(len(wants)):
            t = got[k * 128:(k + 1) * 128, K:].T
            means.append(t[0:1] + (t[1:2] + t[2:3]))
        return got[:, :K].astype(BF16), means

    rows, means = pick([cols[:, g * 128:(g + 1) * 128] for g in range(W // 128)])
    XC[:, :cp, :] = rows.astype(F32).reshape(n, cp, K).astype(BF16)
    for g in range(W // 128):
        XCM[:, g * 128:(g + 1) * 128] = means[g]

    def c_copy(d):
        return to_prod(XC.at[lax.rem(me + d, n)], RC.at[me], c_s.at[0], c_r.at[0], d)

    def k_copy(d):
        return to_prod(XCM, RCM.at[me], k_s.at[0], k_r.at[0], d)

    loop(lambda d: c_copy(d).start())
    loop(lambda d: k_copy(d).start())
    RC[me] = XC[me]
    RCM[me] = XCM[...]

    def ms_copy(d, ic):
        return to_prod(MS.at[0, ic], MS.at[d, ic], ms_s.at[ic], ms_r.at[ic], d)

    def stats(ic, carry):
        i0 = pl.multiple_of(ic * IC, IC)
        u = lax.dot_general(CA[...], TA[pl.ds(i0, IC), :], NT, preferred_element_type=F32)
        UA[...] = u
        m = jnp.maximum(jnp.max(u, axis=0, keepdims=True), 0.0)
        s8 = jnp.sum(jnp.exp(UA[...] - m).reshape(LP // 8, 8, IC), axis=0)
        MS[0, ic, 0:1, :] = m
        MS[0, ic, 1:2, :] = jnp.sum(s8, axis=0, keepdims=True)
        loop(lambda d: ms_copy(d, ic).start())
        return carry

    def cc_copy(d):
        return to_prod(CP, CC.at[me], cc_s.at[0], cc_r.at[0], d)

    span = pad // 2
    part = pl.ds(pl.multiple_of(core * span, span), span)

    def x_copy(d):
        return to_prod(X.at[lax.rem(me + d, n), part], R.at[me, part], x_s.at[0], x_r.at[d], d)

    def m_copy(d):
        return to_prod(XM.at[lax.rem(me + d, n)], RM.at[me], m_s.at[0], m_r.at[0], d)

    def f_copy(d):
        src = lax.rem(me + n - d, n)
        return to_cons(R.at[src, part], R.at[src, part], f_s.at[0], f_r.at[0], partner)

    load_tastes.wait()
    lax.fori_loop(0, 1, stats, 0)
    all_of(RC.at[rest], c_s.at[0], c_r.at[0]).wait()
    all_of(RCM.at[rest], k_s.at[0], k_r.at[0]).wait()
    total = RC[0, :cp, :].astype(F32)
    heads = RCM[0]
    for p in range(1, n):
        total = total + RC[p, :cp, :].astype(F32)
        heads = heads + RCM[p]
    CP[...] = total
    loop(lambda d: cc_copy(d).start())
    CC[me] = CP[...]

    def answer(k, carry):
        sources = [lax.rem(me + n - 2 * k - h, n) for h in range(2)]

        @pl.when(k > 0)
        def _():
            a_copy(2 * k).wait_recv()

        a_copy(2 * k + 1).wait_recv()
        rows, means = pick([asked[src, :, b * 128:(b + 1) * 128] for src in sources for b in range(pb)])
        for h, src in enumerate(sources):
            X[src] = rows[h * pad:(h + 1) * pad]
            for b in range(pb):
                XM[src, :, b * 128:(b + 1) * 128] = means[h * pb + b]

        @pl.when(k > 0)
        def _():
            x_copy(n - 2 * k).start()
            m_copy(n - 2 * k).start()

        x_copy(n - 2 * k - 1).start()
        m_copy(n - 2 * k - 1).start()
        return carry

    lax.fori_loop(0, n // 2, answer, 0)
    all_of(sid.at[rest], a_s.at[0], a_r.at[0]).wait_send()
    R[me] = X[me]
    RM[me] = XM[me]
    lax.fori_loop(1, nc, stats, 0)

    def relay(d):
        x_copy(d).wait_recv()
        f_copy(d).start()

    loop(relay)
    all_of(X.at[rest, part], x_s.at[0], x_r.at[0]).wait_send()

    all_of(RM.at[rest], m_s.at[0], m_r.at[0]).wait()
    all_of(R.at[rest, part], f_s.at[0], f_r.at[0]).wait()

    for p in range(n):
        TB[p * pad:(p + 1) * pad, :K] = R[p]
        for b in range(pb):
            at = p * pad + b * 128
            TB[at:at + 128, K:] = split(turned(RM[p, :, b * 128:(b + 1) * 128]), K)

    def firm(g, carry):
        bands = []
        for h in range(8):
            rows = pl.ds(pl.multiple_of(g * 1024 + h * 128, 128), 128)
            want = turned(fm[:, rows].astype(F32))
            bands.append(jnp.concatenate(
                [
                    jnp.where(want == sid[p, :, b * 128:(b + 1) * 128].astype(F32), 1.0, 0.0).astype(BF16)
                    for p in range(n) for b in range(pb)
                ],
                axis=1,
            ))
        rows = pl.ds(pl.multiple_of(g * 1024, 1024), 1024)
        CF[rows, :] = jnp.dot(jnp.concatenate(bands, axis=0), TB[...], preferred_element_type=F32).astype(BF16)
        return carry

    lax.fori_loop(0, LP // 1024, firm, 0)

    all_of(CC.at[rest], cc_s.at[0], cc_r.at[0]).wait()
    ccv = CC[...].reshape(n * cp, K).astype(BF16)
    cm = jnp.concatenate([turned(heads[:, g * 128:(g + 1) * 128])[:, :1] for g in range(W // 128)], axis=0)

    def weights(ic):
        all_of(MS.at[pl.ds(1, n - 1), ic], ms_s.at[ic], ms_r.at[ic]).wait()
        for w in range(IC // WC):
            i0 = pl.multiple_of(ic * IC + w * WC, WC)
            at = slice(w * WC, (w + 1) * WC)
            peak = MS[0, ic, 0:1, at]
            for d in range(1, n):
                peak = jnp.maximum(peak, MS[d, ic, 0:1, at])
            den = jnp.exp(-peak)
            for d in range(n):
                den = den + MS[d, ic, 1:2, at] * jnp.exp(MS[d, ic, 0:1, at] - peak)
            f = count_products / den
            PK[:, pl.ds(i0, WC)] = peak
            FV[:, pl.ds(i0, WC)] = f
            cu = lax.dot_general(ccv, TA[pl.ds(i0, WC), :K], NT, preferred_element_type=F32) + cm
            w = coef[:, pl.ds(i0, WC)] * (f * jnp.exp(cu - peak))
            WT[pl.ds(i0, WC), :] = w.astype(BF16).T

    def weights_step(ic, carry):
        weights(ic)
        return carry

    lax.fori_loop(0, nc, weights_step, 0)

    def tile_rows(jt):
        return pl.ds(pl.multiple_of(jt * JT, JT), JT)

    def px_copy(jt):
        rows = tile_rows(jt)
        return to_cons(PX.at[rows], PR.at[rows], px_s.at[0], px_r.at[jt], partner)

    def y_copy(jt):
        rows = tile_rows(jt)
        return to_cons(YS.at[rows], YR.at[rows], y_s.at[0], y_r.at[jt], across)

    mine = pl.ds(pl.multiple_of(core * half, half), half)

    def o_copy(jt):
        rows = tile_rows(jt)
        return to_cons(XO.at[rows, mine], XO.at[rows, mine], o_s.at[0], o_r.at[jt], partner)

    theirs = pl.ds(pl.multiple_of((1 - core) * half, half), half)

    def write(jt, which):
        rows = tile_rows(jt)
        return pltpu.make_async_copy(XO.at[rows, which], out.at[rows, which], w_s.at[0])

    def st_copy(d, jt):
        rows = tile_rows(jt)
        return to_cons(
            ST.at[cons, :, rows], ST.at[cons, :, rows], st_s.at[0], st_r.at[0], lax.rem(cons + d, 4)
        )

    def forward(jt):
        rows = tile_rows(jt)
        px_copy(jt).wait_recv()
        YS[rows, :] = (PO[rows, :] + PR[rows, :]).astype(BF16)
        y_copy(jt).start()

    def finish(jt):
        y_copy(jt).wait_recv()
        rows = tile_rows(jt)
        XO[rows, mine] = (YS[rows, :].astype(F32) + YR[rows, :].astype(F32)) / count_consumers
        o_copy(jt).start()
        write(jt, mine).start()

    def gather(jt):
        o_copy(jt).wait_recv()
        write(jt, theirs).start()

    heads_row = cols[...].astype(F32)

    def panel(jt, carry):
        rows = tile_rows(jt)
        UB[...] = lax.dot_general(CF[rows, :], TA[...], NT, preferred_element_type=F32)
        for g in range(JT // GR):
            band = pl.ds(g * GR, GR)
            sh = jnp.zeros((GR, 128), F32)
            dg = jnp.zeros((GR, 128), F32)
            for b in range(LI // 128):
                at = pl.ds(b * 128, 128)
                sc = jnp.exp(UB[band, at] - PK[:, at]) * FV[:, at]
                SCB[band, at] = sc.astype(BF16)
                sh = sh + sc
                dg = dg + sc * coef[:, at]
            SH[band, :] = sh
            DG[band, :] = dg
        acc = jnp.dot(SCB[...], WT[...], preferred_element_type=F32)
        ST[cons, 0:1, rows] = jnp.sum(SH[...].T, axis=0, keepdims=True)
        for d in range(1, 4):
            st_copy(d, jt).start()
        diag = jnp.sum(DG[...], axis=1, keepdims=True)
        ids = jnp.concatenate(
            [
                turned(fm[:, pl.ds(pl.multiple_of(jt * JT + b * 128, 128), 128)].astype(F32))[:, :1]
                for b in range(JT // 128)
            ],
            axis=0,
        )
        acc = acc - jnp.where(ids == heads_row, diag, 0.0)
        first, second = acc[:, :half], acc[:, half:]
        PO[rows, :] = jnp.where(core == 0, first, second)
        PX[rows, :] = jnp.where(core == 0, second, first)
        px_copy(jt).start()

        @pl.when(jt > 0)
        def _():
            forward(jt - 1)

        @pl.when(jt > 3)
        def _():
            finish(jt - 4)

        @pl.when(jt > 4)
        def _():
            gather(jt - 5)

        return carry

    lax.fori_loop(0, nt, panel, 0)
    forward(nt - 1)

    all_of(ST.at[pl.ds(0, 3)], st_s.at[0], st_r.at[0]).wait()
    share = (ST[0] + ST[1] + ST[2] + ST[3]) / count_consumers
    sums = scatter(thirds(share))
    slots = sums[0] + (sums[1] + sums[2])
    for p in range(n):
        for b in range(pb):
            SV[p, :, b * 128:(b + 1) * 128] = slots[p * pb + b:p * pb + b + 1]

    def h_copy(d):
        return to_prod(SV.at[lax.rem(me + d, n)], HV.at[me], h_s.at[0], h_r.at[0], d)

    loop(lambda d: h_copy(d).start())
    HV[me] = SV[me]
    for t in range(max(nt - 4, 0), nt - 1):
        finish(t)
    srow[...] = share
    finish(nt - 1)

    all_of(HV.at[rest], h_s.at[0], h_r.at[0]).wait()
    ids = jnp.concatenate([asked[p] for p in range(n)], axis=1) - base
    idf = ids.astype(F32)
    up = jnp.floor((idf + 0.5) * (1.0 / 128))
    right = jnp.where(idf - up * 128.0 == rows_of((128, n * pad)), 1.0, 0.0).astype(BF16)
    mask = up == rows_of((nb, n * pad))
    back = jnp.concatenate([HV[p] for p in range(n)], axis=1)
    left = jnp.concatenate([jnp.where(mask, p, 0.0) for p in thirds(back)], axis=0).astype(BF16)
    got = lax.dot_general(left, right, NT, preferred_element_type=F32)
    home[...] = got[:nb] + (got[nb:2 * nb] + got[2 * nb:])

    for t in range(max(nt - 5, 0), nt):
        gather(t)
    to_cons(PX, PR, px_s.at[0], px_r.at[0], partner).wait_send()
    to_cons(YS, YR, y_s.at[0], y_r.at[0], across).wait_send()
    to_cons(XO.at[:, mine], XO.at[:, mine], o_s.at[0], o_r.at[0], partner).wait_send()
    pltpu.make_async_copy(XO, out, w_s.at[0]).wait()


def run(n, count_products, count_consumers, fm, cols, chars, mean, tastes, coef):
    LP, K = chars.shape
    LI, W = tastes.shape[0], cols.shape[1]
    half = W // 2
    cp = W // n
    room = -(-cp // 16) * 16
    pad = lanes(LP // n)
    IC, WC, JT, GR = min(1024, LI), min(512, LI), min(256, LP), 32
    nc, nt = LI // IC, LP // JT
    nb, pb = LP // 128, pad // 128
    dma = pltpu.SemaphoreType.DMA
    vm = pltpu.VMEM
    I32 = jnp.int32
    ANY = pl.BlockSpec(memory_space=pltpu.HBM)
    return pl.pallas_call(
        functools.partial(
            step_kernel, n, cp, room, pad, float(count_products), float(count_consumers), IC, WC, JT, GR
        ),
        out_shape=(
            jax.ShapeDtypeStruct((LP, W), F32),
            jax.ShapeDtypeStruct((1, LP), F32),
            jax.ShapeDtypeStruct((nb, 128), F32),
        ),
        in_specs=[VMEM, VMEM, ANY, VMEM, ANY, VMEM],
        out_specs=(ANY, VMEM, VMEM),
        scratch_shapes=[
            vm((LP, 2 * K), BF16), vm((LI, 2 * K), BF16), vm((LP, 2 * K), BF16), vm((n * pad, 2 * K), BF16),
            vm((1, LP), F32), vm((128, LP), BF16),
            vm((n, 1, pad), I32), vm((n, 1, pad), I32),
            vm((n, pad, K), BF16), vm((n, 1, pad), F32), vm((n, pad, K), BF16), vm((n, 1, pad), F32),
            vm((n, room, K), BF16), vm((1, W), F32), vm((n, room, K), BF16), vm((n, 1, W), F32),
            vm((cp, K), F32), vm((n, cp, K), F32),
            vm((LP, IC), F32), vm((n, nc, 2, IC), F32), vm((1, LI), F32), vm((1, LI), F32), vm((LI, W), BF16),
            vm((LP, W), F32), vm((JT, LI), F32), vm((JT, LI), BF16), vm((JT, 128), F32), vm((JT, 128), F32),
            vm((LP, half), F32), vm((LP, half), F32), vm((LP, half), F32),
            vm((LP, half), BF16), vm((LP, half), BF16),
            vm((4, 1, LP), F32), vm((n, 1, pad), F32), vm((n, 1, pad), F32),
        ] + [dma((2,)), dma((1,)), dma((1,)), dma((n,)), dma((1,)), dma((n,))] + [dma((1,))] * 10
        + [dma((nc,))] * 2 + [dma((1,)), dma((nt,))] * 3 + [dma((1,))] * 4,
        compiler_params=pltpu.CompilerParams(collective_id=1, has_side_effects=True, vmem_limit_bytes=LIMIT),
    )(fm, cols, chars, mean, tastes, coef)


def firm_kernel(x, m, srow, home, out, mk, shares):
    block = m.shape[1]
    W = x.shape[1]
    step = pl.program_id(0)

    @pl.when(step == 0)
    def _():
        shares[...] = home[...]

    for b in range(m.shape[0]):
        rows = slice(b * block, (b + 1) * block)
        mh = m[b].astype(BF16)
        pair = jnp.concatenate([mh, (m[b] - mh.astype(F32)).astype(BF16)], axis=1)
        v = x[rows, :]
        h = v.astype(BF16)
        both = jnp.concatenate([h, (v - h.astype(F32)).astype(BF16)], axis=1)
        r = jnp.dot(pair, jnp.concatenate([both, both], axis=0), preferred_element_type=F32)
        out[rows, :] = r[:, :W] + r[:, W:]
        s = srow[:, rows]
        s1 = s.astype(BF16).astype(F32)
        left = jnp.concatenate([jnp.broadcast_to(s1, (8, block)), jnp.broadcast_to(s - s1, (8, block))], axis=0).astype(BF16)
        g = lax.dot_general(jnp.concatenate([left, left], axis=1), pair, NT, preferred_element_type=F32)
        mk[b:b + 1, :] = g[0:1] + g[8:9]


def firms(x, inv, srow, home):
    LP, W = x.shape
    block = inv.shape[1]
    per = min(8, inv.shape[0])
    steps = inv.shape[0] // per
    return pl.pallas_call(
        firm_kernel,
        grid=(steps,),
        out_shape=(
            jax.ShapeDtypeStruct((LP, W), F32),
            jax.ShapeDtypeStruct((inv.shape[0], block), F32),
            jax.ShapeDtypeStruct(home.shape, F32),
        ),
        in_specs=[
            pl.BlockSpec((per * block, W), lambda i: (i, 0)),
            pl.BlockSpec((per, block, block), lambda i: (i, 0, 0)),
            pl.BlockSpec((1, per * block), lambda i: (0, i)),
            pl.BlockSpec(home.shape, lambda i: (0, 0)),
        ],
        out_specs=(
            pl.BlockSpec((per * block, W), lambda i: (i, 0)),
            pl.BlockSpec((per, block), lambda i: (i, 0)),
            pl.BlockSpec(home.shape, lambda i: (0, 0)),
        ),
        compiler_params=pltpu.CompilerParams(vmem_limit_bytes=LIMIT),
    )(x, inv, srow, home)


def body(tastes, price_coef, characteristics, mean_utility, panel_cols, firm_map, inverses):
    n = lax.axis_size("prod")
    LP = characteristics.shape[0]
    jacobian, srow, home = run(
        n, LP * n, tastes.shape[0] * lax.axis_size("cons"),
        firm_map[None, :], panel_cols[None, :], characteristics, mean_utility[None, :],
        tastes, price_coef[None, :],
    )
    response, markup, shares = firms(jacobian, inverses, srow, home)
    return shares.reshape(LP), markup.reshape(LP), response


def solution(mesh):
    return jax.shard_map(
        body,
        mesh=mesh,
        in_specs=(
            P("cons", None),
            P("cons"),
            P("prod", None),
            P("prod"),
            P(),
            P("prod"),
            P("prod", None, None),
        ),
        out_specs=(P("prod"), P("prod"), P("prod", None)),
        check_vma=False,
    )
```

```python
import functools
import jax
import jax.numpy as jnp
from jax import lax
from jax.experimental import pallas as pl
from jax.experimental.pallas import tpu as pltpu
from jax.sharding import PartitionSpec as P

F32 = jnp.float32
BF16 = jnp.bfloat16
NT = (((1,), (1,)), ((), ()))
MESH = pl.DeviceIdType.MESH
VMEM = pl.BlockSpec(memory_space=pltpu.VMEM)
LIMIT = 48 * 1024 * 1024


def lanes(count):
    return -(-count // 128) * 128


def turned(row):
    return jnp.broadcast_to(row, (128, 128)).T


def thirds(x):
    a = x.astype(BF16).astype(F32)
    b = (x - a).astype(BF16).astype(F32)
    return a, b, x - a - b


def split(column, width):
    lane = lax.broadcasted_iota(jnp.int32, (column.shape[0], width), 1)
    a, b, c = thirds(column)
    return jnp.where(lane == 0, a, jnp.where(lane == 1, b, jnp.where(lane == 2, c, 0.0))).astype(BF16)


def rows_of(shape):
    return lax.broadcasted_iota(jnp.int32, shape, 0).astype(F32)


def step_kernel(
    n, cp, room, pad, count_products, count_consumers, IC, WC, JT, GR,
    fm_in, cols_in, chars, mean_in, tastes, coef_in,
    out, srow, home,
    fm, cols, mean, coef,
    CA, TA, CF, TB, KEY, BT, sid, asked,
    X, XM, R, RM, XC, XCM, RC, RCM, CP, CC,
    UA, MS, PK, FV, WT,
    UB, SCB, SH, DG, PO, PX, PR, YS, YR, ST, SV, HV,
    i_s, a_s, a_r, x_s, x_r, f_s, f_r, g_s, g_r, m_s, m_r, c_s, c_r, k_s, k_r, cc_s, cc_r,
    ms_s, ms_r, px_s, px_r, y_s, y_r, o_s, o_r, st_s, st_r, h_s, h_r,
):
    me = lax.axis_index("prod")
    cons = lax.axis_index("cons")
    core = lax.rem(cons, 2)
    partner = cons + 1 - 2 * core
    across = lax.rem(cons + 2, 4)
    LP, K = chars.shape
    LI = tastes.shape[0]
    W = cols.shape[1]
    half = W // 2
    pp = LP // n
    nb, pb = LP // 128, pad // 128
    nc, nw, nt = LI // IC, LI // WC, LP // JT
    base = me * LP

    barrier = pltpu.get_barrier_semaphore()
    for d in range(1, n):
        pl.semaphore_signal(barrier, inc=1, device_id={"prod": lax.rem(me + d, n)}, device_id_type=MESH)
    for d in range(1, 4):
        pl.semaphore_signal(barrier, inc=1, device_id={"cons": lax.rem(cons + d, 4)}, device_id_type=MESH)

    def loop(fn, lo=1):
        def step(d, carry):
            fn(d)
            return carry
        lax.fori_loop(lo, n, step, 0)

    def to_prod(src, dst, s, r, d):
        return pltpu.make_async_remote_copy(
            src, dst, s, r,
            device_id={"prod": lax.rem(me + d, n)}, device_id_type=MESH,
        )

    rest = pl.ds(0, n - 1)

    def all_of(ref, s, r):
        return to_prod(ref, ref, s, r, 1)

    def to_cons(src, dst, s, r, peer):
        return pltpu.make_async_remote_copy(src, dst, s, r, device_id={"cons": peer}, device_id_type=MESH)

    small = [
        pltpu.make_async_copy(src, dst, i_s.at[2 + k])
        for k, (src, dst) in enumerate(((fm_in, fm), (mean_in, mean), (cols_in, cols), (coef_in, coef)))
    ]
    for copy in small:
        copy.start()
    load_chars = pltpu.make_async_copy(chars, CA.at[:, pl.ds(0, K)], i_s.at[0])
    load_tastes = pltpu.make_async_copy(tastes, TA.at[:, pl.ds(0, K)], i_s.at[1])
    load_chars.start()
    load_tastes.start()
    small[0].wait()

    fmf = fm[...].astype(F32)
    source = jnp.floor((fmf + 0.5) * (1.0 / LP))
    local = fmf - source * float(LP)
    owners = rows_of((n, 128))
    marks = jnp.concatenate(
        [jnp.where(source[:, b * 128:(b + 1) * 128] == owners, 1.0, 0.0) for b in range(nb)], axis=0
    )
    at0 = lax.broadcasted_iota(jnp.int32, (128, 128), 0)
    at1 = lax.broadcasted_iota(jnp.int32, (128, 128), 1)
    before = jnp.where(at0 < at1, 1.0, 0.0).astype(BF16)
    inner = jnp.dot(marks.astype(BF16), before, preferred_element_type=F32)
    totals = jnp.dot(marks.astype(BF16), jnp.ones((128, 128), BF16), preferred_element_type=F32)
    q0 = lax.broadcasted_iota(jnp.int32, (nb * n, nb * n), 0).astype(F32)
    q1 = lax.broadcasted_iota(jnp.int32, (nb * n, nb * n), 1).astype(F32)
    b0, b1 = jnp.floor((q0 + 0.5) * (1.0 / n)), jnp.floor((q1 + 0.5) * (1.0 / n))
    earlier = jnp.where((q0 - b0 * n == q1 - b1 * n) & (b1 < b0), 1.0, 0.0).astype(BF16)
    offset = jnp.dot(earlier, totals.astype(BF16), preferred_element_type=F32)
    placed = marks * (inner + offset)
    slot = jnp.concatenate(
        [jnp.sum(placed[b * n:(b + 1) * n], axis=0, keepdims=True) for b in range(nb)], axis=1
    )
    high = jnp.floor((slot + 0.5) * (1.0 / 128))
    KEY[...] = source * float(pb) + high
    BT[...] = jnp.where(slot - high * 128.0 == rows_of((128, LP)), 1.0, 0.0).astype(BF16)

    def scatter(parts):
        mask = KEY[...] == rows_of((n * pb, LP))
        left = jnp.concatenate([jnp.where(mask, p, 0.0) for p in parts], axis=0).astype(BF16)
        got = lax.dot_general(left, BT[...], NT, preferred_element_type=F32)
        return [got[k * n * pb:(k + 1) * n * pb] for k in range(len(parts))]

    upper = jnp.floor((local + 0.5) * (1.0 / 128))
    hi, lo = scatter([upper, local - upper * 128.0])
    q = rows_of((n * pb, 128))
    owner = jnp.floor((q + 0.5) * (1.0 / pb))
    place = (q - owner * pb) * 128.0 + lax.broadcasted_iota(jnp.int32, (n * pb, 128), 1).astype(F32)
    wanted = jnp.where(place < float(pp), owner * float(LP) + hi * 128.0 + lo, -1.0).astype(jnp.int32)
    for p in range(n):
        for b in range(pb):
            sid[p, :, b * 128:(b + 1) * 128] = wanted[p * pb + b:p * pb + b + 1]

    small[1].wait()
    for g in range(nb):
        CA[g * 128:(g + 1) * 128, K:] = split(turned(mean[:, g * 128:(g + 1) * 128]), K)
    TA[:, K:] = jnp.where(lax.broadcasted_iota(jnp.int32, (LI, K), 1) < 3, 1.0, 0.0).astype(BF16)
    pl.semaphore_wait(barrier, n + 2)

    def a_copy(d):
        return to_prod(sid.at[lax.rem(me + d, n)], asked.at[me], a_s.at[0], a_r.at[d], d)

    loop(lambda d: a_copy(d).start())
    asked[me] = sid[me]

    small[2].wait()
    small[3].wait()
    load_chars.wait()

    def pick(wants):
        spot = lax.broadcasted_iota(jnp.int32, (128, 128), 1).astype(F32)
        bands = []
        for w in wants:
            want = turned((w - base).astype(F32))
            bands.append(jnp.concatenate(
                [jnp.where(want == spot + float(b * 128), 1.0, 0.0).astype(BF16) for b in range(nb)], axis=1
            ))
        got = jnp.dot(jnp.concatenate(bands, axis=0), CA[...], preferred_element_type=F32)
        means = []
        for k in range(len(wants)):
            t = got[k * 128:(k + 1) * 128, K:].T
            means.append(t[0:1] + (t[1:2] + t[2:3]))
        return got[:, :K].astype(BF16), means

    rows, means = pick([cols[:, g * 128:(g + 1) * 128] for g in range(W // 128)])
    XC[:, :cp, :] = rows.astype(F32).reshape(n, cp, K).astype(BF16)
    for g in range(W // 128):
        XCM[:, g * 128:(g + 1) * 128] = means[g]

    def c_copy(d):
        return to_prod(XC.at[lax.rem(me + d, n)], RC.at[me], c_s.at[0], c_r.at[0], d)

    def k_copy(d):
        return to_prod(XCM, RCM.at[me], k_s.at[0], k_r.at[0], d)

    loop(lambda d: c_copy(d).start())
    loop(lambda d: k_copy(d).start())
    RC[me] = XC[me]
    RCM[me] = XCM[...]

    def ms_copy(d, ic):
        return to_prod(MS.at[0, ic], MS.at[d, ic], ms_s.at[ic], ms_r.at[ic], d)

    def stats(ic, carry):
        i0 = pl.multiple_of(ic * IC, IC)
        u = lax.dot_general(CA[...], TA[pl.ds(i0, IC), :], NT, preferred_element_type=F32)
        UA[...] = u
        m = jnp.maximum(jnp.max(u, axis=0, keepdims=True), 0.0)
        s8 = jnp.sum(jnp.exp(UA[...] - m).reshape(LP // 8, 8, IC), axis=0)
        MS[0, ic, 0:1, :] = m
        MS[0, ic, 1:2, :] = jnp.sum(s8, axis=0, keepdims=True)
        loop(lambda d: ms_copy(d, ic).start())
        return carry

    def cc_copy(d):
        return to_prod(CP, CC.at[me], cc_s.at[0], cc_r.at[0], d)

    span = pad // 4

    def quarter(c):
        return pl.ds(pl.multiple_of(c * span, span), span)

    part, other = quarter(cons), quarter(across)

    def x_copy(d):
        return to_prod(X.at[lax.rem(me + d, n), part], R.at[me, part], x_s.at[0], x_r.at[d], d)

    def m_copy(d):
        return to_prod(XM.at[lax.rem(me + d, n)], RM.at[me], m_s.at[0], m_r.at[0], d)

    def g_copy(d):
        src = lax.rem(me + n - d, n)
        return to_cons(R.at[src, part], R.at[src, part], g_s.at[0], g_r.at[0], across)

    def f_copy(d, which):
        src = lax.rem(me + n - d, n)
        return to_cons(R.at[src, which], R.at[src, which], f_s.at[0], f_r.at[0], partner)

    load_tastes.wait()
    lax.fori_loop(0, 1, stats, 0)
    def answer(k, carry):
        sources = [lax.rem(me + n - 2 * k - h, n) for h in range(2)]

        @pl.when(k > 0)
        def _():
            a_copy(2 * k).wait_recv()

        a_copy(2 * k + 1).wait_recv()
        rows, means = pick([asked[src, :, b * 128:(b + 1) * 128] for src in sources for b in range(pb)])
        for h, src in enumerate(sources):
            X[src] = rows[h * pad:(h + 1) * pad]
            for b in range(pb):
                XM[src, :, b * 128:(b + 1) * 128] = means[h * pb + b]

        @pl.when(k > 0)
        def _():
            x_copy(n - 2 * k).start()
            m_copy(n - 2 * k).start()

        x_copy(n - 2 * k - 1).start()
        m_copy(n - 2 * k - 1).start()
        return carry

    lax.fori_loop(0, n // 2, answer, 0)
    all_of(sid.at[rest], a_s.at[0], a_r.at[0]).wait_send()
    all_of(RC.at[rest], c_s.at[0], c_r.at[0]).wait()
    all_of(RCM.at[rest], k_s.at[0], k_r.at[0]).wait()
    total = RC[0, :cp, :].astype(F32)
    heads = RCM[0]
    for p in range(1, n):
        total = total + RC[p, :cp, :].astype(F32)
        heads = heads + RCM[p]
    CP[...] = total
    loop(lambda d: cc_copy(d).start())
    CC[me] = CP[...]

    R[me] = X[me]
    RM[me] = XM[me]
    held = max(nc - 1, 1)
    lax.fori_loop(1, held, stats, 0)

    def relay(d):
        x_copy(d).wait_recv()
        g_copy(d).start()
        f_copy(d, part).start()

    loop(relay)
    lax.fori_loop(held, nc, stats, 0)

    all_of(CC.at[rest], cc_s.at[0], cc_r.at[0]).wait()
    ccv = CC[...].reshape(n * cp, K).astype(BF16)
    cm = jnp.concatenate([turned(heads[:, g * 128:(g + 1) * 128])[:, :1] for g in range(W // 128)], axis=0)

    def weights(ic):
        all_of(MS.at[pl.ds(1, n - 1), ic], ms_s.at[ic], ms_r.at[ic]).wait()
        for w in range(IC // WC):
            i0 = pl.multiple_of(ic * IC + w * WC, WC)
            at = slice(w * WC, (w + 1) * WC)
            peak = MS[0, ic, 0:1, at]
            for d in range(1, n):
                peak = jnp.maximum(peak, MS[d, ic, 0:1, at])
            den = jnp.exp(-peak)
            for d in range(n):
                den = den + MS[d, ic, 1:2, at] * jnp.exp(MS[d, ic, 0:1, at] - peak)
            f = count_products / den
            PK[:, pl.ds(i0, WC)] = peak
            FV[:, pl.ds(i0, WC)] = f
            cu = lax.dot_general(ccv, TA[pl.ds(i0, WC), :K], NT, preferred_element_type=F32) + cm
            w = coef[:, pl.ds(i0, WC)] * (f * jnp.exp(cu - peak))
            WT[pl.ds(i0, WC), :] = w.astype(BF16).T

    def weights_step(ic, carry):
        weights(ic)
        return carry

    early = max(held - 1, 0)
    lax.fori_loop(0, early, weights_step, 0)
    all_of(R.at[rest, part], g_s.at[0], g_r.at[0]).wait()
    loop(lambda d: f_copy(d, other).start())
    all_of(X.at[rest, part], x_s.at[0], x_r.at[0]).wait_send()
    lax.fori_loop(early, held, weights_step, 0)

    all_of(RM.at[rest], m_s.at[0], m_r.at[0]).wait()
    all_of(R.at[rest, pl.ds(0, 2 * span)], f_s.at[0], f_r.at[0]).wait()

    for p in range(n):
        TB[p * pad:(p + 1) * pad, :K] = R[p]
        for b in range(pb):
            at = p * pad + b * 128
            TB[at:at + 128, K:] = split(turned(RM[p, :, b * 128:(b + 1) * 128]), K)

    def firm(g, carry):
        bands = []
        for h in range(8):
            rows = pl.ds(pl.multiple_of(g * 1024 + h * 128, 128), 128)
            want = turned(fm[:, rows].astype(F32))
            bands.append(jnp.concatenate(
                [
                    jnp.where(want == sid[p, :, b * 128:(b + 1) * 128].astype(F32), 1.0, 0.0).astype(BF16)
                    for p in range(n) for b in range(pb)
                ],
                axis=1,
            ))
        rows = pl.ds(pl.multiple_of(g * 1024, 1024), 1024)
        CF[rows, :] = jnp.dot(jnp.concatenate(bands, axis=0), TB[...], preferred_element_type=F32).astype(BF16)
        return carry

    lax.fori_loop(0, LP // 1024, firm, 0)

    lax.fori_loop(held, nc, weights_step, 0)


    def tile_rows(jt):
        return pl.ds(pl.multiple_of(jt * JT, JT), JT)

    def px_copy(jt):
        rows = tile_rows(jt)
        return to_cons(PX.at[rows], PR.at[rows], px_s.at[0], px_r.at[jt], partner)

    def y_copy(jt):
        rows = tile_rows(jt)
        return to_cons(YS.at[rows], YR.at[rows], y_s.at[0], y_r.at[jt], across)

    mine = pl.ds(pl.multiple_of(core * half, half), half)

    def o_copy(jt):
        rows = tile_rows(jt)
        return to_cons(out.at[rows, mine], out.at[rows, mine], o_s.at[0], o_r.at[jt], partner)

    def st_copy(d, jt):
        rows = tile_rows(jt)
        return to_cons(
            ST.at[cons, :, rows], ST.at[cons, :, rows], st_s.at[0], st_r.at[0], lax.rem(cons + d, 4)
        )

    def forward(jt):
        rows = tile_rows(jt)
        px_copy(jt).wait_recv()
        YS[rows, :] = (PO[rows, :] + PR[rows, :]).astype(BF16)
        y_copy(jt).start()

    def finish(jt):
        y_copy(jt).wait_recv()
        rows = tile_rows(jt)
        out[rows, mine] = (YS[rows, :].astype(F32) + YR[rows, :].astype(F32)) / count_consumers
        o_copy(jt).start()

    def gather(jt):
        o_copy(jt).wait_recv()

    heads_row = cols[...].astype(F32)

    def panel(jt, carry):
        rows = tile_rows(jt)
        UB[...] = lax.dot_general(CF[rows, :], TA[...], NT, preferred_element_type=F32)
        for g in range(JT // GR):
            band = pl.ds(g * GR, GR)
            sh = jnp.zeros((GR, 128), F32)
            dg = jnp.zeros((GR, 128), F32)
            for b in range(LI // 128):
                at = pl.ds(b * 128, 128)
                sc = jnp.exp(UB[band, at] - PK[:, at]) * FV[:, at]
                SCB[band, at] = sc.astype(BF16)
                sh = sh + sc
                dg = dg + sc * coef[:, at]
            SH[band, :] = sh
            DG[band, :] = dg
        acc = jnp.dot(SCB[...], WT[...], preferred_element_type=F32)
        ST[cons, 0:1, rows] = jnp.sum(SH[...].T, axis=0, keepdims=True)
        for d in range(1, 4):
            st_copy(d, jt).start()
        diag = jnp.sum(DG[...], axis=1, keepdims=True)
        ids = jnp.concatenate(
            [
                turned(fm[:, pl.ds(pl.multiple_of(jt * JT + b * 128, 128), 128)].astype(F32))[:, :1]
                for b in range(JT // 128)
            ],
            axis=0,
        )
        acc = acc - jnp.where(ids == heads_row, diag, 0.0)
        first, second = acc[:, :half], acc[:, half:]
        PO[rows, :] = jnp.where(core == 0, first, second)
        PX[rows, :] = jnp.where(core == 0, second, first)
        px_copy(jt).start()

        @pl.when(jt > 0)
        def _():
            forward(jt - 1)

        @pl.when(jt > 3)
        def _():
            finish(jt - 4)

        @pl.when(jt > 4)
        def _():
            gather(jt - 5)

        return carry

    lax.fori_loop(0, nt, panel, 0)
    forward(nt - 1)
    idf = (jnp.concatenate([asked[p] for p in range(n)], axis=1) - base).astype(F32)
    up = jnp.floor((idf + 0.5) * (1.0 / 128))
    right = jnp.where(idf - up * 128.0 == rows_of((128, n * pad)), 1.0, 0.0).astype(BF16)
    mask = up == rows_of((nb, n * pad))
    all_of(ST.at[pl.ds(0, 3)], st_s.at[0], st_r.at[0]).wait()
    share = (ST[0] + ST[1] + ST[2] + ST[3]) / count_consumers
    sums = scatter(thirds(share))
    slots = sums[0] + (sums[1] + sums[2])
    for p in range(n):
        for b in range(pb):
            SV[p, :, b * 128:(b + 1) * 128] = slots[p * pb + b:p * pb + b + 1]

    def h_copy(d):
        return to_prod(SV.at[lax.rem(me + d, n)], HV.at[me], h_s.at[0], h_r.at[0], d)

    loop(lambda d: h_copy(d).start())
    HV[me] = SV[me]
    srow[...] = share
    for t in range(max(nt - 4, 0), nt):
        finish(t)
    for t in range(max(nt - 5, 0), nt):
        gather(t)
    all_of(HV.at[rest], h_s.at[0], h_r.at[0]).wait()
    back = jnp.concatenate([HV[p] for p in range(n)], axis=1)
    left = jnp.concatenate([jnp.where(mask, p, 0.0) for p in thirds(back)], axis=0).astype(BF16)
    got = lax.dot_general(left, right, NT, preferred_element_type=F32)
    home[...] = got[:nb] + (got[nb:2 * nb] + got[2 * nb:])
    to_cons(PX, PR, px_s.at[0], px_r.at[0], partner).wait_send()
    to_cons(YS, YR, y_s.at[0], y_r.at[0], across).wait_send()
    to_cons(out.at[:, mine], out.at[:, mine], o_s.at[0], o_r.at[0], partner).wait_send()


def run(n, count_products, count_consumers, fm, cols, chars, mean, tastes, coef):
    LP, K = chars.shape
    LI, W = tastes.shape[0], cols.shape[1]
    half = W // 2
    cp = W // n
    room = -(-cp // 16) * 16
    pad = lanes(LP // n)
    IC, WC, JT, GR = min(1024, LI), min(512, LI), min(256, LP), 32
    nc, nt = LI // IC, LP // JT
    nb, pb = LP // 128, pad // 128
    dma = pltpu.SemaphoreType.DMA
    vm = pltpu.VMEM
    I32 = jnp.int32
    ANY = pl.BlockSpec(memory_space=pltpu.HBM)
    return pl.pallas_call(
        functools.partial(
            step_kernel, n, cp, room, pad, float(count_products), float(count_consumers), IC, WC, JT, GR
        ),
        out_shape=(
            jax.ShapeDtypeStruct((LP, W), F32),
            jax.ShapeDtypeStruct((1, LP), F32),
            jax.ShapeDtypeStruct((nb, 128), F32),
        ),
        in_specs=[ANY] * 6,
        out_specs=(VMEM,) * 3,
        scratch_shapes=[
            vm((1, LP), I32), vm((1, W), I32), vm((1, LP), F32), vm((1, LI), F32),
            vm((LP, 2 * K), BF16), vm((LI, 2 * K), BF16), vm((LP, 2 * K), BF16), vm((n * pad, 2 * K), BF16),
            vm((1, LP), F32), vm((128, LP), BF16),
            vm((n, 1, pad), I32), vm((n, 1, pad), I32),
            vm((n, pad, K), BF16), vm((n, 1, pad), F32), vm((n, pad, K), BF16), vm((n, 1, pad), F32),
            vm((n, room, K), BF16), vm((1, W), F32), vm((n, room, K), BF16), vm((n, 1, W), F32),
            vm((cp, K), F32), vm((n, cp, K), F32),
            vm((LP, IC), F32), vm((n, nc, 2, IC), F32), vm((1, LI), F32), vm((1, LI), F32), vm((LI, W), BF16),
            vm((JT, LI), F32), vm((JT, LI), BF16), vm((JT, 128), F32), vm((JT, 128), F32),
            vm((LP, half), F32), vm((LP, half), F32), vm((LP, half), F32),
            vm((LP, half), BF16), vm((LP, half), BF16),
            vm((4, 1, LP), F32), vm((n, 1, pad), F32), vm((n, 1, pad), F32),
        ] + [dma((6,)), dma((1,)), dma((n,)), dma((1,)), dma((n,))] + [dma((1,))] * 12
        + [dma((nc,))] * 2 + [dma((1,)), dma((nt,))] * 3 + [dma((1,))] * 4,
        compiler_params=pltpu.CompilerParams(collective_id=1, has_side_effects=True, vmem_limit_bytes=LIMIT),
    )(*[pltpu.with_memory_space_constraint(v, pltpu.HBM) for v in (fm, cols, chars, mean, tastes, coef)])


def firm_kernel(x, m, srow, home, out, mk, shares):
    block = m.shape[1]
    W = x.shape[1]
    step = pl.program_id(0)

    @pl.when(step == 0)
    def _():
        shares[...] = home[...]

    for b in range(m.shape[0]):
        rows = slice(b * block, (b + 1) * block)
        mh = m[b].astype(BF16)
        pair = jnp.concatenate([mh, (m[b] - mh.astype(F32)).astype(BF16)], axis=1)
        v = x[rows, :]
        h = v.astype(BF16)
        both = jnp.concatenate([h, (v - h.astype(F32)).astype(BF16)], axis=1)
        r = jnp.dot(pair, jnp.concatenate([both, both], axis=0), preferred_element_type=F32)
        out[rows, :] = r[:, :W] + r[:, W:]
        s = srow[:, rows]
        s1 = s.astype(BF16).astype(F32)
        left = jnp.concatenate([jnp.broadcast_to(s1, (8, block)), jnp.broadcast_to(s - s1, (8, block))], axis=0).astype(BF16)
        g = lax.dot_general(jnp.concatenate([left, left], axis=1), pair, NT, preferred_element_type=F32)
        mk[pl.ds(step * m.shape[0] + b, 1), :] = g[0:1] + g[8:9]


def firms(x, inv, srow, home):
    LP, W = x.shape
    block = inv.shape[1]
    per = min(8, inv.shape[0])
    steps = inv.shape[0] // per
    return pl.pallas_call(
        firm_kernel,
        grid=(steps,),
        out_shape=(
            jax.ShapeDtypeStruct((LP, W), F32),
            jax.ShapeDtypeStruct((inv.shape[0], block), F32),
            jax.ShapeDtypeStruct(home.shape, F32),
        ),
        in_specs=[
            pl.BlockSpec((per * block, W), lambda i: (i, 0)),
            pl.BlockSpec((per, block, block), lambda i: (i, 0, 0)),
            pl.BlockSpec((1, per * block), lambda i: (0, i)),
            pl.BlockSpec(home.shape, lambda i: (0, 0)),
        ],
        out_specs=(
            pl.BlockSpec((per * block, W), lambda i: (i, 0)),
            pl.BlockSpec((inv.shape[0], block), lambda i: (0, 0)),
            pl.BlockSpec(home.shape, lambda i: (0, 0)),
        ),
        compiler_params=pltpu.CompilerParams(vmem_limit_bytes=16 * 1024 * 1024),
    )(x, inv, srow, home)


def body(tastes, price_coef, characteristics, mean_utility, panel_cols, firm_map, inverses):
    n = lax.axis_size("prod")
    LP = characteristics.shape[0]
    jacobian, srow, home = run(
        n, LP * n, tastes.shape[0] * lax.axis_size("cons"),
        firm_map[None, :], panel_cols[None, :], characteristics, mean_utility[None, :],
        tastes, price_coef[None, :],
    )
    response, markup, shares = firms(jacobian, inverses, srow, home)
    return shares.reshape(LP), markup.reshape(LP), response


def solution(mesh):
    return jax.shard_map(
        body,
        mesh=mesh,
        in_specs=(
            P("cons", None),
            P("cons"),
            P("prod", None),
            P("prod"),
            P(),
            P("prod"),
            P("prod", None, None),
        ),
        out_specs=(P("prod"), P("prod"), P("prod", None)),
        check_vma=False,
    )
```

```python
import functools
import jax
import jax.numpy as jnp
from jax import lax
from jax.experimental import pallas as pl
from jax.experimental.pallas import tpu as pltpu
from jax.sharding import PartitionSpec as P

F32 = jnp.float32
BF16 = jnp.bfloat16
NT = (((1,), (1,)), ((), ()))
MESH = pl.DeviceIdType.MESH
VMEM = pl.BlockSpec(memory_space=pltpu.VMEM)
LIMIT = 48 * 1024 * 1024


def lanes(count):
    return -(-count // 128) * 128


def turned(row):
    return jnp.broadcast_to(row, (128, 128)).T


def thirds(x):
    a = x.astype(BF16).astype(F32)
    b = (x - a).astype(BF16).astype(F32)
    return a, b, x - a - b


def split(column, width):
    lane = lax.broadcasted_iota(jnp.int32, (column.shape[0], width), 1)
    a, b, c = thirds(column)
    return jnp.where(lane == 0, a, jnp.where(lane == 1, b, jnp.where(lane == 2, c, 0.0))).astype(BF16)


def rows_of(shape):
    return lax.broadcasted_iota(jnp.int32, shape, 0).astype(F32)


def step_kernel(
    n, cp, room, pad, count_products, count_consumers, IC, WC, JT, GR,
    fm_in, cols_in, chars, mean_in, tastes, coef_in, inv_in,
    out, pairs, mk, home,
    fm, cols, mean, coef, inv,
    CA, TA, CF, TB, KEY, BT, sid, asked,
    IDC, RT, UP, X, XM, R, RM, XC, XCM, RC, RCM, CP, CC,
    UA, MS, PK, FV, WT,
    UB, SCB, SH, DG, PO, PX, PR, YS, YR, ST, SV, HV,
    i_s, a_s, a_r, x_s, x_r, f_s, f_r, g_s, g_r, m_s, m_r, c_s, c_r, k_s, k_r, cc_s, cc_r,
    ms_s, ms_r, px_s, px_r, y_s, y_r, o_s, o_r, st_s, st_r, h_s, h_r,
):
    me = lax.axis_index("prod")
    cons = lax.axis_index("cons")
    core = lax.rem(cons, 2)
    partner = cons + 1 - 2 * core
    across = lax.rem(cons + 2, 4)
    LP, K = chars.shape
    LI = tastes.shape[0]
    W = cols.shape[1]
    half = W // 2
    block = inv.shape[1]
    pp = LP // n
    nb, pb = LP // 128, pad // 128
    nc, nw, nt = LI // IC, LI // WC, LP // JT
    base = me * LP

    barrier = pltpu.get_barrier_semaphore()
    for d in range(1, n):
        pl.semaphore_signal(barrier, inc=1, device_id={"prod": lax.rem(me + d, n)}, device_id_type=MESH)
    for d in range(1, 4):
        pl.semaphore_signal(barrier, inc=1, device_id={"cons": lax.rem(cons + d, 4)}, device_id_type=MESH)

    def loop(fn, lo=1):
        def step(d, carry):
            fn(d)
            return carry
        lax.fori_loop(lo, n, step, 0)

    def to_prod(src, dst, s, r, d):
        return pltpu.make_async_remote_copy(
            src, dst, s, r,
            device_id={"prod": lax.rem(me + d, n)}, device_id_type=MESH,
        )

    rest = pl.ds(0, n - 1)

    def all_of(ref, s, r):
        return to_prod(ref, ref, s, r, 1)

    def to_cons(src, dst, s, r, peer):
        return pltpu.make_async_remote_copy(src, dst, s, r, device_id={"cons": peer}, device_id_type=MESH)

    small = [
        pltpu.make_async_copy(src, dst, i_s.at[2 + k])
        for k, (src, dst) in enumerate(((fm_in, fm), (mean_in, mean), (cols_in, cols), (coef_in, coef)))
    ]
    for copy in small:
        copy.start()
    load_chars = pltpu.make_async_copy(chars, CA.at[:, pl.ds(0, K)], i_s.at[0])
    load_tastes = pltpu.make_async_copy(tastes, TA.at[:, pl.ds(0, K)], i_s.at[1])
    load_chars.start()
    load_tastes.start()
    load_inv = pltpu.make_async_copy(inv_in, inv, i_s.at[6])
    load_inv.start()
    small[0].wait()

    fmf = fm[...].astype(F32)
    source = jnp.floor((fmf + 0.5) * (1.0 / LP))
    local = fmf - source * float(LP)
    owners = rows_of((n, 128))
    marks = jnp.concatenate(
        [jnp.where(source[:, b * 128:(b + 1) * 128] == owners, 1.0, 0.0) for b in range(nb)], axis=0
    )
    at0 = lax.broadcasted_iota(jnp.int32, (128, 128), 0)
    at1 = lax.broadcasted_iota(jnp.int32, (128, 128), 1)
    before = jnp.where(at0 < at1, 1.0, 0.0).astype(BF16)
    inner = jnp.dot(marks.astype(BF16), before, preferred_element_type=F32)
    totals = jnp.dot(marks.astype(BF16), jnp.ones((128, 128), BF16), preferred_element_type=F32)
    q0 = lax.broadcasted_iota(jnp.int32, (nb * n, nb * n), 0).astype(F32)
    q1 = lax.broadcasted_iota(jnp.int32, (nb * n, nb * n), 1).astype(F32)
    b0, b1 = jnp.floor((q0 + 0.5) * (1.0 / n)), jnp.floor((q1 + 0.5) * (1.0 / n))
    earlier = jnp.where((q0 - b0 * n == q1 - b1 * n) & (b1 < b0), 1.0, 0.0).astype(BF16)
    offset = jnp.dot(earlier, totals.astype(BF16), preferred_element_type=F32)
    placed = marks * (inner + offset)
    slot = jnp.concatenate(
        [jnp.sum(placed[b * n:(b + 1) * n], axis=0, keepdims=True) for b in range(nb)], axis=1
    )
    high = jnp.floor((slot + 0.5) * (1.0 / 128))
    KEY[...] = source * float(pb) + high
    BT[...] = jnp.where(slot - high * 128.0 == rows_of((128, LP)), 1.0, 0.0).astype(BF16)

    def scatter(parts):
        mask = KEY[...] == rows_of((n * pb, LP))
        left = jnp.concatenate([jnp.where(mask, p, 0.0) for p in parts], axis=0).astype(BF16)
        got = lax.dot_general(left, BT[...], NT, preferred_element_type=F32)
        return [got[k * n * pb:(k + 1) * n * pb] for k in range(len(parts))]

    upper = jnp.floor((local + 0.5) * (1.0 / 128))
    hi, lo = scatter([upper, local - upper * 128.0])
    q = rows_of((n * pb, 128))
    owner = jnp.floor((q + 0.5) * (1.0 / pb))
    place = (q - owner * pb) * 128.0 + lax.broadcasted_iota(jnp.int32, (n * pb, 128), 1).astype(F32)
    wanted = jnp.where(place < float(pp), owner * float(LP) + hi * 128.0 + lo, -1.0).astype(jnp.int32)
    for p in range(n):
        for b in range(pb):
            sid[p, :, b * 128:(b + 1) * 128] = wanted[p * pb + b:p * pb + b + 1]

    small[1].wait()
    for g in range(nb):
        CA[g * 128:(g + 1) * 128, K:] = split(turned(mean[:, g * 128:(g + 1) * 128]), K)
    TA[:, K:] = jnp.where(lax.broadcasted_iota(jnp.int32, (LI, K), 1) < 3, 1.0, 0.0).astype(BF16)
    pl.semaphore_wait(barrier, n + 2)

    def a_copy(d):
        return to_prod(sid.at[lax.rem(me + d, n)], asked.at[me], a_s.at[0], a_r.at[d], d)

    loop(lambda d: a_copy(d).start())
    asked[me] = sid[me]

    small[2].wait()
    small[3].wait()
    load_chars.wait()

    def pick(wants):
        spot = lax.broadcasted_iota(jnp.int32, (128, 128), 1).astype(F32)
        bands = []
        for w in wants:
            want = turned((w - base).astype(F32))
            bands.append(jnp.concatenate(
                [jnp.where(want == spot + float(b * 128), 1.0, 0.0).astype(BF16) for b in range(nb)], axis=1
            ))
        got = jnp.dot(jnp.concatenate(bands, axis=0), CA[...], preferred_element_type=F32)
        means = []
        for k in range(len(wants)):
            t = got[k * 128:(k + 1) * 128, K:].T
            means.append(t[0:1] + (t[1:2] + t[2:3]))
        return got[:, :K].astype(BF16), means

    rows, means = pick([cols[:, g * 128:(g + 1) * 128] for g in range(W // 128)])
    XC[:, :cp, :] = rows.astype(F32).reshape(n, cp, K).astype(BF16)
    for g in range(W // 128):
        XCM[:, g * 128:(g + 1) * 128] = means[g]

    def c_copy(d):
        return to_prod(XC.at[lax.rem(me + d, n)], RC.at[me], c_s.at[0], c_r.at[0], d)

    def k_copy(d):
        return to_prod(XCM, RCM.at[me], k_s.at[0], k_r.at[0], d)

    loop(lambda d: c_copy(d).start())
    loop(lambda d: k_copy(d).start())
    RC[me] = XC[me]
    RCM[me] = XCM[...]

    def ms_copy(d, ic):
        return to_prod(MS.at[0, ic], MS.at[d, ic], ms_s.at[ic], ms_r.at[ic], d)

    def stats(ic, carry):
        i0 = pl.multiple_of(ic * IC, IC)
        u = lax.dot_general(CA[...], TA[pl.ds(i0, IC), :], NT, preferred_element_type=F32)
        UA[...] = u
        m = jnp.maximum(jnp.max(u, axis=0, keepdims=True), 0.0)
        s8 = jnp.sum(jnp.exp(UA[...] - m).reshape(LP // 8, 8, IC), axis=0)
        MS[0, ic, 0:1, :] = m
        MS[0, ic, 1:2, :] = jnp.sum(s8, axis=0, keepdims=True)
        loop(lambda d: ms_copy(d, ic).start())
        return carry

    def cc_copy(d):
        return to_prod(CP, CC.at[me], cc_s.at[0], cc_r.at[0], d)

    span = pad // 4

    def quarter(c):
        return pl.ds(pl.multiple_of(c * span, span), span)

    part, other = quarter(cons), quarter(across)

    def x_copy(d):
        return to_prod(X.at[lax.rem(me + d, n)], R.at[me, part], x_s.at[0], x_r.at[d], d)

    def m_copy(d):
        return to_prod(XM.at[lax.rem(me + d, n)], RM.at[me], m_s.at[0], m_r.at[0], d)

    def g_copy(d, batch):
        src = lax.rem(me + n - d, n)
        return to_cons(R.at[src, part], R.at[src, part], g_s.at[0], g_r.at[batch], across)

    def f_copy(d, which):
        src = lax.rem(me + n - d, n)
        return to_cons(R.at[src, which], R.at[src, which], f_s.at[0], f_r.at[0], partner)

    load_tastes.wait()
    lax.fori_loop(0, 1, stats, 0)
    loop(lambda d: a_copy(d).wait_recv())
    for p in range(n):
        for b in range(pb):
            IDC[p, b * 128:(b + 1) * 128, :] = turned((asked[p, :, b * 128:(b + 1) * 128] - base).astype(F32))
    spot = lax.broadcasted_iota(jnp.int32, (1, 128), 1).astype(F32)

    def hots(want):
        return jnp.concatenate(
            [jnp.where(want == spot + float(b * 128), 1.0, 0.0).astype(BF16) for b in range(nb)], axis=1
        )

    asks = jnp.concatenate([hots(IDC[p, part, :]) for p in range(n)] + [hots(IDC[me])], axis=0)
    got = jnp.dot(asks, CA[:, :K], preferred_element_type=F32).astype(BF16)
    for p in range(n):
        X[p] = got[p * span:(p + 1) * span]
    R[me] = got[n * span:]
    loop(lambda d: x_copy(d).start())
    idf = (jnp.concatenate([asked[p] for p in range(n)], axis=1) - base).astype(F32)
    up = jnp.floor((idf + 0.5) * (1.0 / 128))
    RT[...] = jnp.where(idf - up * 128.0 == rows_of((128, n * pad)), 1.0, 0.0).astype(BF16)
    UP[...] = up
    grid = jnp.concatenate([mean[:, b * 128:(b + 1) * 128] for b in range(nb)], axis=0)
    found = jnp.dot(jnp.concatenate(thirds(grid), axis=0).astype(BF16), RT[...], preferred_element_type=F32)
    found = found[:nb] + (found[nb:2 * nb] + found[2 * nb:])
    means = jnp.sum(jnp.where(up == rows_of((nb, n * pad)), found, 0.0), axis=0, keepdims=True)
    for p in range(n):
        XM[p] = means[:, p * pad:(p + 1) * pad]
    loop(lambda d: m_copy(d).start())
    all_of(sid.at[rest], a_s.at[0], a_r.at[0]).wait_send()
    all_of(RC.at[rest], c_s.at[0], c_r.at[0]).wait()
    all_of(RCM.at[rest], k_s.at[0], k_r.at[0]).wait()
    total = RC[0, :cp, :].astype(F32)
    heads = RCM[0]
    for p in range(1, n):
        total = total + RC[p, :cp, :].astype(F32)
        heads = heads + RCM[p]
    CP[:cp, :] = total.astype(BF16)
    loop(lambda d: cc_copy(d).start())
    CC[me] = CP[...]

    RM[me] = XM[me]
    held = max(nc - 1, 1)
    lax.fori_loop(1, held, stats, 0)

    first = n // 2

    def pass_on(batch, lo, hi):
        def step(d, carry):
            x_copy(d).wait_recv()
            f_copy(d, part).start()
            return carry
        lax.fori_loop(lo, hi, step, 0)
        def across_step(d, carry):
            g_copy(d, batch).start()
            return carry
        lax.fori_loop(lo, hi, across_step, 0)

    def hand_over(batch, lo, hi):
        all_of(R.at[pl.ds(0, hi - lo), part], g_s.at[0], g_r.at[batch]).wait_recv()
        def step(d, carry):
            f_copy(d, other).start()
            return carry
        lax.fori_loop(lo, hi, step, 0)

    pass_on(0, 1, first)
    pass_on(1, first, n)
    lax.fori_loop(held, nc, stats, 0)
    hand_over(0, 1, first)

    all_of(CC.at[rest], cc_s.at[0], cc_r.at[0]).wait()
    ccv = CC[:, :cp, :].astype(F32).reshape(n * cp, K).astype(BF16)
    cm = jnp.concatenate([turned(heads[:, g * 128:(g + 1) * 128])[:, :1] for g in range(W // 128)], axis=0)

    def weights(ic):
        all_of(MS.at[pl.ds(1, n - 1), ic], ms_s.at[ic], ms_r.at[ic]).wait()
        for w in range(IC // WC):
            i0 = pl.multiple_of(ic * IC + w * WC, WC)
            at = slice(w * WC, (w + 1) * WC)
            peak = MS[0, ic, 0:1, at]
            for d in range(1, n):
                peak = jnp.maximum(peak, MS[d, ic, 0:1, at])
            den = jnp.exp(-peak)
            for d in range(n):
                den = den + MS[d, ic, 1:2, at] * jnp.exp(MS[d, ic, 0:1, at] - peak)
            f = count_products / den
            PK[:, pl.ds(i0, WC)] = peak
            FV[:, pl.ds(i0, WC)] = f
            cu = lax.dot_general(ccv, TA[pl.ds(i0, WC), :K], NT, preferred_element_type=F32) + cm
            w = coef[:, pl.ds(i0, WC)] * (f * jnp.exp(cu - peak))
            WT[pl.ds(i0, WC), :] = w.astype(BF16).T

    def weights_step(ic, carry):
        weights(ic)
        return carry

    lax.fori_loop(0, min(1, held), weights_step, 0)
    hand_over(1, first, n)
    lax.fori_loop(min(1, held), held, weights_step, 0)
    all_of(R.at[rest, part], g_s.at[0], g_r.at[0]).wait_send()
    all_of(X.at[rest], x_s.at[0], x_r.at[0]).wait_send()

    all_of(RM.at[rest], m_s.at[0], m_r.at[0]).wait()
    for p in range(n):
        for b in range(pb):
            at = p * pad + b * 128
            TB[at:at + 128, K:] = split(turned(RM[p, :, b * 128:(b + 1) * 128]), K)
    all_of(R.at[rest, pl.ds(0, 2 * span)], f_s.at[0], f_r.at[0]).wait()

    for p in range(n):
        TB[p * pad:(p + 1) * pad, :K] = R[p]

    def firm(g, carry):
        bands = []
        for h in range(8):
            rows = pl.ds(pl.multiple_of(g * 1024 + h * 128, 128), 128)
            want = turned(fm[:, rows].astype(F32))
            bands.append(jnp.concatenate(
                [
                    jnp.where(want == sid[p, :, b * 128:(b + 1) * 128].astype(F32), 1.0, 0.0).astype(BF16)
                    for p in range(n) for b in range(pb)
                ],
                axis=1,
            ))
        rows = pl.ds(pl.multiple_of(g * 1024, 1024), 1024)
        CF[rows, :] = jnp.dot(jnp.concatenate(bands, axis=0), TB[...], preferred_element_type=F32).astype(BF16)
        return carry

    lax.fori_loop(0, LP // 1024, firm, 0)

    lax.fori_loop(held, nc, weights_step, 0)


    def tile_rows(jt):
        return pl.ds(pl.multiple_of(jt * JT, JT), JT)

    def px_copy(jt):
        rows = tile_rows(jt)
        return to_cons(PX.at[rows], PR.at[rows], px_s.at[0], px_r.at[jt], partner)

    def y_copy(jt):
        rows = tile_rows(jt)
        return to_cons(YS.at[rows], YR.at[rows], y_s.at[0], y_r.at[jt], across)

    mine = [pl.ds(pl.multiple_of(core * half + k * W, half), half) for k in range(2)]

    def o_copy(jt, k):
        rows = tile_rows(jt)
        return to_cons(out.at[rows, mine[k]], out.at[rows, mine[k]], o_s.at[0], o_r.at[jt], partner)

    def st_copy(d, jt):
        rows = tile_rows(jt)
        return to_cons(
            ST.at[cons, :, rows], ST.at[cons, :, rows], st_s.at[0], st_r.at[0], lax.rem(cons + d, 4)
        )

    def forward(jt):
        rows = tile_rows(jt)
        px_copy(jt).wait_recv()
        YS[rows, :] = (PO[rows, :] + PR[rows, :]).astype(BF16)
        y_copy(jt).start()

    def finish(jt):
        y_copy(jt).wait_recv()
        rows = tile_rows(jt)
        x = (YS[rows, :].astype(F32) + YR[rows, :].astype(F32)) / count_consumers
        h = x.astype(BF16)
        out[rows, mine[0]] = h
        out[rows, mine[1]] = (x - h.astype(F32)).astype(BF16)
        o_copy(jt, 0).start()
        o_copy(jt, 1).start()

    def gather(jt):
        both = out.at[tile_rows(jt), pl.ds(0, W)]
        to_cons(both, both, o_s.at[0], o_r.at[jt], partner).wait_recv()

    heads_row = cols[...].astype(F32)

    def panel(jt, carry):
        rows = tile_rows(jt)
        UB[...] = lax.dot_general(CF[rows, :], TA[...], NT, preferred_element_type=F32)
        for g in range(JT // GR):
            band = pl.ds(g * GR, GR)
            sh = jnp.zeros((GR, 128), F32)
            dg = jnp.zeros((GR, 128), F32)
            for b in range(LI // 128):
                at = pl.ds(b * 128, 128)
                sc = jnp.exp(UB[band, at] - PK[:, at]) * FV[:, at]
                SCB[band, at] = sc.astype(BF16)
                sh = sh + sc
                dg = dg + sc * coef[:, at]
            SH[band, :] = sh
            DG[band, :] = dg
        acc = jnp.dot(SCB[...], WT[...], preferred_element_type=F32)
        ST[cons, 0:1, rows] = jnp.sum(SH[...].T, axis=0, keepdims=True)
        diag = jnp.sum(DG[...], axis=1, keepdims=True)
        ids = jnp.concatenate(
            [
                turned(fm[:, pl.ds(pl.multiple_of(jt * JT + b * 128, 128), 128)].astype(F32))[:, :1]
                for b in range(JT // 128)
            ],
            axis=0,
        )
        acc = acc - jnp.where(ids == heads_row, diag, 0.0)
        first, second = acc[:, :half], acc[:, half:]
        PO[rows, :] = jnp.where(core == 0, first, second)
        PX[rows, :] = jnp.where(core == 0, second, first)
        px_copy(jt).start()
        for d in range(1, 4):
            st_copy(d, jt).start()

        @pl.when(jt > 0)
        def _():
            forward(jt - 1)

        @pl.when(jt > 3)
        def _():
            finish(jt - 4)

        @pl.when(jt > 4)
        def _():
            gather(jt - 5)

        return carry

    lax.fori_loop(0, nt, panel, 0)
    forward(nt - 1)
    all_of(ST.at[pl.ds(0, 3)], st_s.at[0], st_r.at[0]).wait()
    share = (ST[0] + ST[1] + ST[2] + ST[3]) / count_consumers
    sums = scatter(thirds(share))
    slots = sums[0] + (sums[1] + sums[2])
    for p in range(n):
        for b in range(pb):
            SV[p, :, b * 128:(b + 1) * 128] = slots[p * pb + b:p * pb + b + 1]

    def h_copy(d):
        return to_prod(SV.at[lax.rem(me + d, n)], HV.at[me], h_s.at[0], h_r.at[0], d)

    loop(lambda d: h_copy(d).start())
    HV[me] = SV[me]
    load_inv.wait()
    s1 = share.astype(BF16).astype(F32)
    s2 = share - s1
    for b in range(inv.shape[0]):
        m = inv[b]
        mh = m.astype(BF16)
        pair = jnp.concatenate([mh, (m - mh.astype(F32)).astype(BF16)], axis=1)
        pairs[b] = pair
        at = slice(b * block, (b + 1) * block)
        left = jnp.concatenate(
            [jnp.broadcast_to(s1[:, at], (8, block)), jnp.broadcast_to(s2[:, at], (8, block))], axis=0
        ).astype(BF16)
        g = lax.dot_general(jnp.concatenate([left, left], axis=1), pair, NT, preferred_element_type=F32)
        mk[b:b + 1, :] = g[0:1] + g[8:9]
    for t in range(max(nt - 4, 0), nt):
        finish(t)
    for t in range(max(nt - 5, 0), nt):
        gather(t)
    all_of(HV.at[rest], h_s.at[0], h_r.at[0]).wait()
    back = jnp.concatenate([HV[p] for p in range(n)], axis=1)
    mask = UP[...] == rows_of((nb, n * pad))
    left = jnp.concatenate([jnp.where(mask, p, 0.0) for p in thirds(back)], axis=0).astype(BF16)
    got = lax.dot_general(left, RT[...], NT, preferred_element_type=F32)
    home[...] = got[:nb] + (got[nb:2 * nb] + got[2 * nb:])
    to_cons(PX, PR, px_s.at[0], px_r.at[0], partner).wait_send()
    to_cons(YS, YR, y_s.at[0], y_r.at[0], across).wait_send()
    to_cons(out.at[:, pl.ds(0, W)], out.at[:, pl.ds(0, W)], o_s.at[0], o_r.at[0], partner).wait_send()


def run(n, count_products, count_consumers, fm, cols, chars, mean, tastes, coef, inv):
    LP, K = chars.shape
    LI, W = tastes.shape[0], cols.shape[1]
    half = W // 2
    cp = W // n
    room = -(-cp // 16) * 16
    pad = lanes(LP // n)
    IC, WC, JT, GR = min(1024, LI), min(512, LI), min(256, LP), 32
    nc, nt = LI // IC, LP // JT
    nb, pb = LP // 128, pad // 128
    count, block = inv.shape[0], inv.shape[1]
    dma = pltpu.SemaphoreType.DMA
    vm = pltpu.VMEM
    I32 = jnp.int32
    ANY = pl.BlockSpec(memory_space=pltpu.HBM)
    return pl.pallas_call(
        functools.partial(
            step_kernel, n, cp, room, pad, float(count_products), float(count_consumers), IC, WC, JT, GR
        ),
        out_shape=(
            jax.ShapeDtypeStruct((LP, 2 * W), BF16),
            jax.ShapeDtypeStruct((count, block, 2 * block), BF16),
            jax.ShapeDtypeStruct((count, block), F32),
            jax.ShapeDtypeStruct((nb, 128), F32),
        ),
        in_specs=[ANY] * 7,
        out_specs=(VMEM,) * 4,
        scratch_shapes=[
            vm((1, LP), I32), vm((1, W), I32), vm((1, LP), F32), vm((1, LI), F32), vm(inv.shape, F32),
            vm((LP, 2 * K), BF16), vm((LI, 2 * K), BF16), vm((LP, 2 * K), BF16), vm((n * pad, 2 * K), BF16),
            vm((1, LP), F32), vm((128, LP), BF16),
            vm((n, 1, pad), I32), vm((n, 1, pad), I32),
            vm((n, pad, 128), F32), vm((128, n * pad), BF16), vm((1, n * pad), F32),
            vm((n, pad // 4, K), BF16), vm((n, 1, pad), F32), vm((n, pad, K), BF16), vm((n, 1, pad), F32),
            vm((n, room, K), BF16), vm((1, W), F32), vm((n, room, K), BF16), vm((n, 1, W), F32),
            vm((room, K), BF16), vm((n, room, K), BF16),
            vm((LP, IC), F32), vm((n, nc, 2, IC), F32), vm((1, LI), F32), vm((1, LI), F32), vm((LI, W), BF16),
            vm((JT, LI), F32), vm((JT, LI), BF16), vm((JT, 128), F32), vm((JT, 128), F32),
            vm((LP, half), F32), vm((LP, half), F32), vm((LP, half), F32),
            vm((LP, half), BF16), vm((LP, half), BF16),
            vm((4, 1, LP), F32), vm((n, 1, pad), F32), vm((n, 1, pad), F32),
        ] + [dma((7,)), dma((1,)), dma((n,)), dma((1,)), dma((n,))] + [dma((1,))] * 3 + [dma((2,))] + [dma((1,))] * 8
        + [dma((nc,))] * 2 + [dma((1,)), dma((nt,))] * 3 + [dma((1,))] * 4,
        compiler_params=pltpu.CompilerParams(collective_id=1, has_side_effects=True, vmem_limit_bytes=LIMIT),
    )(*[pltpu.with_memory_space_constraint(v, pltpu.HBM) for v in (fm, cols, chars, mean, tastes, coef, inv)])


def firm_kernel(x, pairs, mk, home, out, markup, shares):
    block = pairs.shape[1]
    W = out.shape[1]

    @pl.when(pl.program_id(0) == 0)
    def _():
        shares[...] = home[...]
        markup[...] = mk[...]

    for b in range(pairs.shape[0]):
        rows = slice(b * block, (b + 1) * block)
        both = x[rows, :]
        r = jnp.dot(pairs[b], jnp.concatenate([both, both], axis=0), preferred_element_type=F32)
        out[rows, :] = r[:, :W] + r[:, W:]


def firms(x, pairs, mk, home):
    LP, W = x.shape[0], x.shape[1] // 2
    count, block = pairs.shape[0], pairs.shape[1]
    per = min(8, count)
    whole = lambda a: pl.BlockSpec(a.shape, lambda i: (0, 0))
    return pl.pallas_call(
        firm_kernel,
        grid=(count // per,),
        out_shape=(
            jax.ShapeDtypeStruct((LP, W), F32),
            jax.ShapeDtypeStruct(mk.shape, F32),
            jax.ShapeDtypeStruct(home.shape, F32),
        ),
        in_specs=[
            pl.BlockSpec((per * block, 2 * W), lambda i: (i, 0)),
            pl.BlockSpec((per, block, 2 * block), lambda i: (i, 0, 0)),
            whole(mk),
            whole(home),
        ],
        out_specs=(pl.BlockSpec((per * block, W), lambda i: (i, 0)), whole(mk), whole(home)),
        compiler_params=pltpu.CompilerParams(vmem_limit_bytes=16 * 1024 * 1024),
    )(x, pairs, mk, home)


def body(tastes, price_coef, characteristics, mean_utility, panel_cols, firm_map, inverses):
    n = lax.axis_size("prod")
    LP = characteristics.shape[0]
    jacobian, pairs, mk, home = run(
        n, LP * n, tastes.shape[0] * lax.axis_size("cons"),
        firm_map[None, :], panel_cols[None, :], characteristics, mean_utility[None, :],
        tastes, price_coef[None, :], inverses,
    )
    response, markup, shares = firms(jacobian, pairs, mk, home)
    return shares.reshape(LP), markup.reshape(LP), response


def solution(mesh):
    return jax.shard_map(
        body,
        mesh=mesh,
        in_specs=(
            P("cons", None),
            P("cons"),
            P("prod", None),
            P("prod"),
            P(),
            P("prod"),
            P("prod", None, None),
        ),
        out_specs=(P("prod"), P("prod"), P("prod", None)),
        check_vma=False,
    )
```

```python
import functools
import jax
import jax.numpy as jnp
from jax import lax
from jax.experimental import pallas as pl
from jax.experimental.pallas import tpu as pltpu
from jax.sharding import PartitionSpec as P

F32 = jnp.float32
BF16 = jnp.bfloat16
NT = (((1,), (1,)), ((), ()))
MESH = pl.DeviceIdType.MESH
VMEM = pl.BlockSpec(memory_space=pltpu.VMEM)
LIMIT = 48 * 1024 * 1024


def lanes(count):
    return -(-count // 128) * 128


def turned(row):
    return jnp.broadcast_to(row, (128, 128)).T


def thirds(x):
    a = x.astype(BF16).astype(F32)
    b = (x - a).astype(BF16).astype(F32)
    return a, b, x - a - b


def split(column, width):
    lane = lax.broadcasted_iota(jnp.int32, (column.shape[0], width), 1)
    a, b, c = thirds(column)
    return jnp.where(lane == 0, a, jnp.where(lane == 1, b, jnp.where(lane == 2, c, 0.0))).astype(BF16)


def rows_of(shape):
    return lax.broadcasted_iota(jnp.int32, shape, 0).astype(F32)


def step_kernel(
    n, cp, room, pad, count_products, count_consumers, IC, WC, JT, GR,
    fm_in, cols_in, chars, mean_in, tastes, coef_in, inv_in,
    out, pairs, mk, home,
    fm, cols, mean, coef, inv,
    CA, TA, CF, TB, KEY, BT, sid, asked,
    IDC, RT, UP, X, XM, R, RM, XC, XCM, RC, RCM, CP, CC,
    UA, MS, PK, FV, WT,
    UB, SCB, SH, DG, PO, PX, PR, YS, YR, ST, SV, HV,
    i_s, a_s, a_r, x_s, x_r, f_s, f_r, g_s, g_r, m_s, m_r, c_s, c_r, k_s, k_r, cc_s, cc_r,
    ms_s, ms_r, px_s, px_r, y_s, y_r, o_s, o_r, st_s, st_r, h_s, h_r,
):
    me = lax.axis_index("prod")
    cons = lax.axis_index("cons")
    core = lax.rem(cons, 2)
    partner = cons + 1 - 2 * core
    across = lax.rem(cons + 2, 4)
    LP, K = chars.shape
    LI = tastes.shape[0]
    W = cols.shape[1]
    half = W // 2
    block = inv.shape[1]
    pp = LP // n
    nb, pb = LP // 128, pad // 128
    nc, nw, nt = LI // IC, LI // WC, LP // JT
    base = me * LP

    barrier = pltpu.get_barrier_semaphore()
    for d in range(1, n):
        pl.semaphore_signal(barrier, inc=1, device_id={"prod": lax.rem(me + d, n)}, device_id_type=MESH)
    for d in range(1, 4):
        pl.semaphore_signal(barrier, inc=1, device_id={"cons": lax.rem(cons + d, 4)}, device_id_type=MESH)

    def loop(fn, lo=1):
        def step(d, carry):
            fn(d)
            return carry
        lax.fori_loop(lo, n, step, 0)

    def to_prod(src, dst, s, r, d):
        return pltpu.make_async_remote_copy(
            src, dst, s, r,
            device_id={"prod": lax.rem(me + d, n)}, device_id_type=MESH,
        )

    rest = pl.ds(0, n - 1)

    def all_of(ref, s, r):
        return to_prod(ref, ref, s, r, 1)

    def to_cons(src, dst, s, r, peer):
        return pltpu.make_async_remote_copy(src, dst, s, r, device_id={"cons": peer}, device_id_type=MESH)

    small = [
        pltpu.make_async_copy(src, dst, i_s.at[2 + k])
        for k, (src, dst) in enumerate(((fm_in, fm), (mean_in, mean), (cols_in, cols), (coef_in, coef)))
    ]
    for copy in small:
        copy.start()
    load_chars = pltpu.make_async_copy(chars, CA.at[:, pl.ds(0, K)], i_s.at[0])
    load_tastes = pltpu.make_async_copy(tastes, TA.at[:, pl.ds(0, K)], i_s.at[1])
    load_chars.start()
    load_tastes.start()
    load_inv = pltpu.make_async_copy(inv_in, inv, i_s.at[6])
    load_inv.start()

    TA[:, K:] = jnp.where(lax.broadcasted_iota(jnp.int32, (LI, K), 1) < 3, 1.0, 0.0).astype(BF16)
    at0 = lax.broadcasted_iota(jnp.int32, (128, 128), 0)
    at1 = lax.broadcasted_iota(jnp.int32, (128, 128), 1)
    before = jnp.where(at0 < at1, 1.0, 0.0).astype(BF16)
    q0 = lax.broadcasted_iota(jnp.int32, (nb * n, nb * n), 0).astype(F32)
    q1 = lax.broadcasted_iota(jnp.int32, (nb * n, nb * n), 1).astype(F32)
    b0, b1 = jnp.floor((q0 + 0.5) * (1.0 / n)), jnp.floor((q1 + 0.5) * (1.0 / n))
    earlier = jnp.where((q0 - b0 * n == q1 - b1 * n) & (b1 < b0), 1.0, 0.0).astype(BF16)
    small[0].wait()
    fmf = fm[...].astype(F32)
    source = jnp.floor((fmf + 0.5) * (1.0 / LP))
    local = fmf - source * float(LP)
    owners = rows_of((n, 128))
    marks = jnp.concatenate(
        [jnp.where(source[:, b * 128:(b + 1) * 128] == owners, 1.0, 0.0) for b in range(nb)], axis=0
    )
    inner = jnp.dot(marks.astype(BF16), before, preferred_element_type=F32)
    totals = jnp.dot(marks.astype(BF16), jnp.ones((128, 128), BF16), preferred_element_type=F32)
    offset = jnp.dot(earlier, totals.astype(BF16), preferred_element_type=F32)
    placed = marks * (inner + offset)
    slot = jnp.concatenate(
        [jnp.sum(placed[b * n:(b + 1) * n], axis=0, keepdims=True) for b in range(nb)], axis=1
    )
    high = jnp.floor((slot + 0.5) * (1.0 / 128))
    KEY[...] = source * float(pb) + high
    BT[...] = jnp.where(slot - high * 128.0 == rows_of((128, LP)), 1.0, 0.0).astype(BF16)

    def scatter(parts):
        mask = KEY[...] == rows_of((n * pb, LP))
        left = jnp.concatenate([jnp.where(mask, p, 0.0) for p in parts], axis=0).astype(BF16)
        got = lax.dot_general(left, BT[...], NT, preferred_element_type=F32)
        return [got[k * n * pb:(k + 1) * n * pb] for k in range(len(parts))]

    upper = jnp.floor((local + 0.5) * (1.0 / 128))
    hi, lo = scatter([upper, local - upper * 128.0])
    q = rows_of((n * pb, 128))
    owner = jnp.floor((q + 0.5) * (1.0 / pb))
    place = (q - owner * pb) * 128.0 + lax.broadcasted_iota(jnp.int32, (n * pb, 128), 1).astype(F32)
    wanted = jnp.where(place < float(pp), owner * float(LP) + hi * 128.0 + lo, -1.0).astype(jnp.int32)
    for p in range(n):
        for b in range(pb):
            sid[p, :, b * 128:(b + 1) * 128] = wanted[p * pb + b:p * pb + b + 1]

    small[1].wait()
    for g in range(nb):
        CA[g * 128:(g + 1) * 128, K:] = split(turned(mean[:, g * 128:(g + 1) * 128]), K)
    pl.semaphore_wait(barrier, n + 2)

    def a_copy(d):
        return to_prod(sid.at[lax.rem(me + d, n)], asked.at[me], a_s.at[0], a_r.at[d], d)

    loop(lambda d: a_copy(d).start())
    asked[me] = sid[me]

    small[2].wait()
    small[3].wait()
    load_chars.wait()

    def pick(wants):
        spot = lax.broadcasted_iota(jnp.int32, (128, 128), 1).astype(F32)
        bands = []
        for w in wants:
            want = turned((w - base).astype(F32))
            bands.append(jnp.concatenate(
                [jnp.where(want == spot + float(b * 128), 1.0, 0.0).astype(BF16) for b in range(nb)], axis=1
            ))
        got = jnp.dot(jnp.concatenate(bands, axis=0), CA[...], preferred_element_type=F32)
        means = []
        for k in range(len(wants)):
            t = got[k * 128:(k + 1) * 128, K:].T
            means.append(t[0:1] + (t[1:2] + t[2:3]))
        return got[:, :K].astype(BF16), means

    rows, means = pick([cols[:, g * 128:(g + 1) * 128] for g in range(W // 128)])
    XC[:, :cp, :] = rows.astype(F32).reshape(n, cp, K).astype(BF16)
    for g in range(W // 128):
        XCM[:, g * 128:(g + 1) * 128] = means[g]

    def c_copy(d):
        return to_prod(XC.at[lax.rem(me + d, n)], RC.at[me], c_s.at[0], c_r.at[0], d)

    def k_copy(d):
        return to_prod(XCM, RCM.at[me], k_s.at[0], k_r.at[0], d)

    loop(lambda d: c_copy(d).start())
    loop(lambda d: k_copy(d).start())
    RC[me] = XC[me]
    RCM[me] = XCM[...]

    def ms_copy(d, ic):
        return to_prod(MS.at[0, ic], MS.at[d, ic], ms_s.at[ic], ms_r.at[ic], d)

    def stats(ic, carry):
        i0 = pl.multiple_of(ic * IC, IC)
        u = lax.dot_general(CA[...], TA[pl.ds(i0, IC), :], NT, preferred_element_type=F32)
        UA[...] = u
        m = jnp.maximum(jnp.max(u, axis=0, keepdims=True), 0.0)
        s8 = jnp.sum(jnp.exp(UA[...] - m).reshape(LP // 8, 8, IC), axis=0)
        MS[0, ic, 0:1, :] = m
        MS[0, ic, 1:2, :] = jnp.sum(s8, axis=0, keepdims=True)
        loop(lambda d: ms_copy(d, ic).start())
        return carry

    def cc_copy(d):
        return to_prod(CP, CC.at[me], cc_s.at[0], cc_r.at[0], d)

    span = pad // 4

    def quarter(c):
        return pl.ds(pl.multiple_of(c * span, span), span)

    part, other = quarter(cons), quarter(across)

    def x_copy(d):
        return to_prod(X.at[lax.rem(me + d, n)], R.at[me, part], x_s.at[0], x_r.at[d], d)

    def m_copy(d):
        return to_prod(XM.at[lax.rem(me + d, n)], RM.at[me], m_s.at[0], m_r.at[0], d)

    def g_copy(d, batch):
        src = lax.rem(me + n - d, n)
        return to_cons(R.at[src, part], R.at[src, part], g_s.at[0], g_r.at[batch], across)

    def f_copy(d, which):
        src = lax.rem(me + n - d, n)
        return to_cons(R.at[src, which], R.at[src, which], f_s.at[0], f_r.at[0], partner)

    load_tastes.wait()
    lax.fori_loop(0, 1, stats, 0)
    loop(lambda d: a_copy(d).wait_recv())
    for p in range(n):
        for b in range(pb):
            IDC[p, b * 128:(b + 1) * 128, :] = turned((asked[p, :, b * 128:(b + 1) * 128] - base).astype(F32))
    spot = lax.broadcasted_iota(jnp.int32, (1, 128), 1).astype(F32)

    def hots(want):
        return jnp.concatenate(
            [jnp.where(want == spot + float(b * 128), 1.0, 0.0).astype(BF16) for b in range(nb)], axis=1
        )

    asks = jnp.concatenate([hots(IDC[p, part, :]) for p in range(n)] + [hots(IDC[me])], axis=0)
    got = jnp.dot(asks, CA[:, :K], preferred_element_type=F32).astype(BF16)
    for p in range(n):
        X[p] = got[p * span:(p + 1) * span]
    R[me] = got[n * span:]
    loop(lambda d: x_copy(d).start())
    idf = (jnp.concatenate([asked[p] for p in range(n)], axis=1) - base).astype(F32)
    up = jnp.floor((idf + 0.5) * (1.0 / 128))
    RT[...] = jnp.where(idf - up * 128.0 == rows_of((128, n * pad)), 1.0, 0.0).astype(BF16)
    UP[...] = up
    grid = jnp.concatenate([mean[:, b * 128:(b + 1) * 128] for b in range(nb)], axis=0)
    found = jnp.dot(jnp.concatenate(thirds(grid), axis=0).astype(BF16), RT[...], preferred_element_type=F32)
    found = found[:nb] + (found[nb:2 * nb] + found[2 * nb:])
    means = jnp.sum(jnp.where(up == rows_of((nb, n * pad)), found, 0.0), axis=0, keepdims=True)
    for p in range(n):
        XM[p] = means[:, p * pad:(p + 1) * pad]
    loop(lambda d: m_copy(d).start())
    all_of(sid.at[rest], a_s.at[0], a_r.at[0]).wait_send()
    all_of(RC.at[rest], c_s.at[0], c_r.at[0]).wait()
    all_of(RCM.at[rest], k_s.at[0], k_r.at[0]).wait()
    total = RC[0, :cp, :].astype(F32)
    heads = RCM[0]
    for p in range(1, n):
        total = total + RC[p, :cp, :].astype(F32)
        heads = heads + RCM[p]
    CP[:cp, :] = total.astype(BF16)
    loop(lambda d: cc_copy(d).start())
    CC[me] = CP[...]

    RM[me] = XM[me]
    held = max(nc - 1, 1)
    lax.fori_loop(1, held, stats, 0)

    first = n // 2

    def pass_on(batch, lo, hi):
        def step(d, carry):
            x_copy(d).wait_recv()
            f_copy(d, part).start()
            return carry
        lax.fori_loop(lo, hi, step, 0)
        def across_step(d, carry):
            g_copy(d, batch).start()
            return carry
        lax.fori_loop(lo, hi, across_step, 0)

    def hand_over(batch, lo, hi):
        all_of(R.at[pl.ds(0, hi - lo), part], g_s.at[0], g_r.at[batch]).wait_recv()
        def step(d, carry):
            f_copy(d, other).start()
            return carry
        lax.fori_loop(lo, hi, step, 0)

    pass_on(0, 1, first)
    pass_on(1, first, n)
    lax.fori_loop(held, nc, stats, 0)
    hand_over(0, 1, first)

    all_of(CC.at[rest], cc_s.at[0], cc_r.at[0]).wait()
    ccv = CC[:, :cp, :].astype(F32).reshape(n * cp, K).astype(BF16)
    cm = jnp.concatenate([turned(heads[:, g * 128:(g + 1) * 128])[:, :1] for g in range(W // 128)], axis=0)

    def weights(ic):
        all_of(MS.at[pl.ds(1, n - 1), ic], ms_s.at[ic], ms_r.at[ic]).wait()
        for w in range(IC // WC):
            i0 = pl.multiple_of(ic * IC + w * WC, WC)
            at = slice(w * WC, (w + 1) * WC)
            peak = MS[0, ic, 0:1, at]
            for d in range(1, n):
                peak = jnp.maximum(peak, MS[d, ic, 0:1, at])
            den = jnp.exp(-peak)
            for d in range(n):
                den = den + MS[d, ic, 1:2, at] * jnp.exp(MS[d, ic, 0:1, at] - peak)
            f = count_products / den
            PK[:, pl.ds(i0, WC)] = peak
            FV[:, pl.ds(i0, WC)] = f
            cu = lax.dot_general(ccv, TA[pl.ds(i0, WC), :K], NT, preferred_element_type=F32) + cm
            w = coef[:, pl.ds(i0, WC)] * (f * jnp.exp(cu - peak))
            WT[pl.ds(i0, WC), :] = w.astype(BF16).T

    def weights_step(ic, carry):
        weights(ic)
        return carry

    lax.fori_loop(0, min(1, held), weights_step, 0)
    hand_over(1, first, n)
    lax.fori_loop(min(1, held), held, weights_step, 0)
    all_of(R.at[rest, part], g_s.at[0], g_r.at[0]).wait_send()
    all_of(X.at[rest], x_s.at[0], x_r.at[0]).wait_send()

    all_of(RM.at[rest], m_s.at[0], m_r.at[0]).wait()
    for p in range(n):
        for b in range(pb):
            at = p * pad + b * 128
            TB[at:at + 128, K:] = split(turned(RM[p, :, b * 128:(b + 1) * 128]), K)
    all_of(R.at[rest, pl.ds(0, 2 * span)], f_s.at[0], f_r.at[0]).wait()

    for p in range(n):
        TB[p * pad:(p + 1) * pad, :K] = R[p]

    def firm(g, carry):
        bands = []
        for h in range(8):
            rows = pl.ds(pl.multiple_of(g * 1024 + h * 128, 128), 128)
            want = turned(fm[:, rows].astype(F32))
            bands.append(jnp.concatenate(
                [
                    jnp.where(want == sid[p, :, b * 128:(b + 1) * 128].astype(F32), 1.0, 0.0).astype(BF16)
                    for p in range(n) for b in range(pb)
                ],
                axis=1,
            ))
        rows = pl.ds(pl.multiple_of(g * 1024, 1024), 1024)
        CF[rows, :] = jnp.dot(jnp.concatenate(bands, axis=0), TB[...], preferred_element_type=F32).astype(BF16)
        return carry

    lax.fori_loop(0, LP // 1024, firm, 0)

    lax.fori_loop(held, nc, weights_step, 0)


    def tile_rows(jt):
        return pl.ds(pl.multiple_of(jt * JT, JT), JT)

    def px_copy(jt):
        rows = tile_rows(jt)
        return to_cons(PX.at[rows], PR.at[rows], px_s.at[0], px_r.at[jt], partner)

    def y_copy(jt):
        rows = tile_rows(jt)
        return to_cons(YS.at[rows], YR.at[rows], y_s.at[0], y_r.at[jt], across)

    mine = [pl.ds(pl.multiple_of(core * half + k * W, half), half) for k in range(2)]

    def o_copy(jt, k):
        rows = tile_rows(jt)
        return to_cons(out.at[rows, mine[k]], out.at[rows, mine[k]], o_s.at[0], o_r.at[0], partner)

    def st_copy(d, jt):
        rows = tile_rows(jt)
        return to_cons(
            ST.at[cons, :, rows], ST.at[cons, :, rows], st_s.at[0], st_r.at[0], lax.rem(cons + d, 4)
        )

    def forward(jt):
        rows = tile_rows(jt)
        px_copy(jt).wait_recv()
        YS[rows, :] = (PO[rows, :] + PR[rows, :]).astype(BF16)
        y_copy(jt).start()

    def finish(jt):
        y_copy(jt).wait_recv()
        rows = tile_rows(jt)
        x = (YS[rows, :].astype(F32) + YR[rows, :].astype(F32)) / count_consumers
        h = x.astype(BF16)
        out[rows, mine[0]] = h
        out[rows, mine[1]] = (x - h.astype(F32)).astype(BF16)
        o_copy(jt, 0).start()
        o_copy(jt, 1).start()

    heads_row = cols[...].astype(F32)

    def panel(jt, carry):
        rows = tile_rows(jt)
        UB[...] = lax.dot_general(CF[rows, :], TA[...], NT, preferred_element_type=F32)
        for g in range(JT // GR):
            band = pl.ds(g * GR, GR)
            sh = jnp.zeros((GR, 128), F32)
            dg = jnp.zeros((GR, 128), F32)
            for b in range(LI // 128):
                at = pl.ds(b * 128, 128)
                sc = jnp.exp(UB[band, at] - PK[:, at]) * FV[:, at]
                SCB[band, at] = sc.astype(BF16)
                sh = sh + sc
                dg = dg + sc * coef[:, at]
            SH[band, :] = sh
            DG[band, :] = dg
        acc = jnp.dot(SCB[...], WT[...], preferred_element_type=F32)
        ST[cons, 0:1, rows] = jnp.sum(SH[...].T, axis=0, keepdims=True)
        diag = jnp.sum(DG[...], axis=1, keepdims=True)
        ids = jnp.concatenate(
            [
                turned(fm[:, pl.ds(pl.multiple_of(jt * JT + b * 128, 128), 128)].astype(F32))[:, :1]
                for b in range(JT // 128)
            ],
            axis=0,
        )
        acc = acc - jnp.where(ids == heads_row, diag, 0.0)
        first, second = acc[:, :half], acc[:, half:]
        PO[rows, :] = jnp.where(core == 0, first, second)
        PX[rows, :] = jnp.where(core == 0, second, first)
        px_copy(jt).start()
        for d in range(1, 4):
            st_copy(d, jt).start()

        @pl.when(jt > 0)
        def _():
            forward(jt - 1)

        @pl.when(jt > 3)
        def _():
            finish(jt - 4)

        return carry

    lax.fori_loop(0, nt, panel, 0)
    forward(nt - 1)
    all_of(ST.at[pl.ds(0, 3)], st_s.at[0], st_r.at[0]).wait()
    share = (ST[0] + ST[1] + ST[2] + ST[3]) / count_consumers
    sums = scatter(thirds(share))
    slots = sums[0] + (sums[1] + sums[2])
    for p in range(n):
        for b in range(pb):
            SV[p, :, b * 128:(b + 1) * 128] = slots[p * pb + b:p * pb + b + 1]

    def h_copy(d):
        return to_prod(SV.at[lax.rem(me + d, n)], HV.at[me], h_s.at[0], h_r.at[0], d)

    loop(lambda d: h_copy(d).start())
    HV[me] = SV[me]
    load_inv.wait()
    s1 = share.astype(BF16).astype(F32)
    s2 = share - s1
    for b in range(inv.shape[0]):
        m = inv[b]
        mh = m.astype(BF16)
        pair = jnp.concatenate([mh, (m - mh.astype(F32)).astype(BF16)], axis=1)
        pairs[b] = pair
        at = slice(b * block, (b + 1) * block)
        left = jnp.concatenate(
            [jnp.broadcast_to(s1[:, at], (8, block)), jnp.broadcast_to(s2[:, at], (8, block))], axis=0
        ).astype(BF16)
        g = lax.dot_general(jnp.concatenate([left, left], axis=1), pair, NT, preferred_element_type=F32)
        mk[b:b + 1, :] = g[0:1] + g[8:9]
    for t in range(max(nt - 4, 0), nt):
        finish(t)
    all_of(HV.at[rest], h_s.at[0], h_r.at[0]).wait()
    back = jnp.concatenate([HV[p] for p in range(n)], axis=1)
    mask = UP[...] == rows_of((nb, n * pad))
    left = jnp.concatenate([jnp.where(mask, p, 0.0) for p in thirds(back)], axis=0).astype(BF16)
    got = lax.dot_general(left, RT[...], NT, preferred_element_type=F32)
    home[...] = got[:nb] + (got[nb:2 * nb] + got[2 * nb:])
    to_cons(PX, PR, px_s.at[0], px_r.at[0], partner).wait_send()
    to_cons(YS, YR, y_s.at[0], y_r.at[0], across).wait_send()
    to_cons(out.at[:, pl.ds(0, W)], out.at[:, pl.ds(0, W)], o_s.at[0], o_r.at[0], partner).wait()


def run(n, count_products, count_consumers, fm, cols, chars, mean, tastes, coef, inv):
    LP, K = chars.shape
    LI, W = tastes.shape[0], cols.shape[1]
    half = W // 2
    cp = W // n
    room = -(-cp // 16) * 16
    pad = lanes(LP // n)
    IC, WC, JT, GR = min(1024, LI), min(512, LI), min(256, LP), 32
    nc, nt = LI // IC, LP // JT
    nb, pb = LP // 128, pad // 128
    count, block = inv.shape[0], inv.shape[1]
    dma = pltpu.SemaphoreType.DMA
    vm = pltpu.VMEM
    I32 = jnp.int32
    ANY = pl.BlockSpec(memory_space=pltpu.HBM)
    return pl.pallas_call(
        functools.partial(
            step_kernel, n, cp, room, pad, float(count_products), float(count_consumers), IC, WC, JT, GR
        ),
        out_shape=(
            jax.ShapeDtypeStruct((LP, 2 * W), BF16),
            jax.ShapeDtypeStruct((count, block, 2 * block), BF16),
            jax.ShapeDtypeStruct((count, block), F32),
            jax.ShapeDtypeStruct((nb, 128), F32),
        ),
        in_specs=[ANY] * 7,
        out_specs=(VMEM,) * 4,
        scratch_shapes=[
            vm((1, LP), I32), vm((1, W), I32), vm((1, LP), F32), vm((1, LI), F32), vm(inv.shape, F32),
            vm((LP, 2 * K), BF16), vm((LI, 2 * K), BF16), vm((LP, 2 * K), BF16), vm((n * pad, 2 * K), BF16),
            vm((1, LP), F32), vm((128, LP), BF16),
            vm((n, 1, pad), I32), vm((n, 1, pad), I32),
            vm((n, pad, 128), F32), vm((128, n * pad), BF16), vm((1, n * pad), F32),
            vm((n, pad // 4, K), BF16), vm((n, 1, pad), F32), vm((n, pad, K), BF16), vm((n, 1, pad), F32),
            vm((n, room, K), BF16), vm((1, W), F32), vm((n, room, K), BF16), vm((n, 1, W), F32),
            vm((room, K), BF16), vm((n, room, K), BF16),
            vm((LP, IC), F32), vm((n, nc, 2, IC), F32), vm((1, LI), F32), vm((1, LI), F32), vm((LI, W), BF16),
            vm((JT, LI), F32), vm((JT, LI), BF16), vm((JT, 128), F32), vm((JT, 128), F32),
            vm((LP, half), F32), vm((LP, half), F32), vm((LP, half), F32),
            vm((LP, half), BF16), vm((LP, half), BF16),
            vm((4, 1, LP), F32), vm((n, 1, pad), F32), vm((n, 1, pad), F32),
        ] + [dma((7,)), dma((1,)), dma((n,)), dma((1,)), dma((n,))] + [dma((1,))] * 3 + [dma((2,))] + [dma((1,))] * 8
        + [dma((nc,))] * 2 + [dma((1,)), dma((nt,))] * 2 + [dma((1,))] * 6,
        compiler_params=pltpu.CompilerParams(collective_id=1, has_side_effects=True, vmem_limit_bytes=LIMIT),
    )(*[pltpu.with_memory_space_constraint(v, pltpu.HBM) for v in (fm, cols, chars, mean, tastes, coef, inv)])


def firm_kernel(x, pairs, mk, home, out, markup, shares):
    block = pairs.shape[1]
    W = out.shape[1]

    @pl.when(pl.program_id(0) == 0)
    def _():
        shares[...] = home[...]
        markup[...] = mk[...]

    per = out.shape[0] // block
    for b in range(per):
        rows = slice(b * block, (b + 1) * block)
        at = pl.program_id(0) * per + b
        both = x[pl.ds(pl.multiple_of(at * block, block), block), :]
        r = jnp.dot(pairs[at], jnp.concatenate([both, both], axis=0), preferred_element_type=F32)
        out[rows, :] = r[:, :W] + r[:, W:]


def firms(x, pairs, mk, home):
    LP, W = x.shape[0], x.shape[1] // 2
    count, block = pairs.shape[0], pairs.shape[1]
    per = min(8, count)
    whole = lambda a: pl.BlockSpec(a.shape, lambda i: (0, 0))
    return pl.pallas_call(
        firm_kernel,
        grid=(count // per,),
        out_shape=(
            jax.ShapeDtypeStruct((LP, W), F32),
            jax.ShapeDtypeStruct(mk.shape, F32),
            jax.ShapeDtypeStruct(home.shape, F32),
        ),
        in_specs=[
            VMEM,
            VMEM,
            whole(mk),
            whole(home),
        ],
        out_specs=(pl.BlockSpec((per * block, W), lambda i: (i, 0)), whole(mk), whole(home)),
        compiler_params=pltpu.CompilerParams(vmem_limit_bytes=16 * 1024 * 1024),
    )(x, pairs, mk, home)


def body(tastes, price_coef, characteristics, mean_utility, panel_cols, firm_map, inverses):
    n = lax.axis_size("prod")
    LP = characteristics.shape[0]
    jacobian, pairs, mk, home = run(
        n, LP * n, tastes.shape[0] * lax.axis_size("cons"),
        firm_map[None, :], panel_cols[None, :], characteristics, mean_utility[None, :],
        tastes, price_coef[None, :], inverses,
    )
    response, markup, shares = firms(jacobian, pairs, mk, home)
    return shares.reshape(LP), markup.reshape(LP), response


def solution(mesh):
    return jax.shard_map(
        body,
        mesh=mesh,
        in_specs=(
            P("cons", None),
            P("cons"),
            P("prod", None),
            P("prod"),
            P(),
            P("prod"),
            P("prod", None, None),
        ),
        out_specs=(P("prod"), P("prod"), P("prod", None)),
        check_vma=False,
    )
```

```python
import functools
import jax
import jax.numpy as jnp
from jax import lax
from jax.experimental import pallas as pl
from jax.experimental.pallas import tpu as pltpu
from jax.sharding import PartitionSpec as P

F32 = jnp.float32
BF16 = jnp.bfloat16
NT = (((1,), (1,)), ((), ()))
MESH = pl.DeviceIdType.MESH
VMEM = pl.BlockSpec(memory_space=pltpu.VMEM)
LIMIT = 48 * 1024 * 1024


def lanes(count):
    return -(-count // 128) * 128


def turned(row):
    return jnp.broadcast_to(row, (128, 128)).T


def thirds(x):
    a = x.astype(BF16).astype(F32)
    b = (x - a).astype(BF16).astype(F32)
    return a, b, x - a - b


def split(column, width):
    lane = lax.broadcasted_iota(jnp.int32, (column.shape[0], width), 1)
    a, b, c = thirds(column)
    return jnp.where(lane == 0, a, jnp.where(lane == 1, b, jnp.where(lane == 2, c, 0.0))).astype(BF16)


def rows_of(shape):
    return lax.broadcasted_iota(jnp.int32, shape, 0).astype(F32)


def step_kernel(
    n, cp, room, pad, count_products, count_consumers, IC, WC, JT, GR,
    fm_in, cols_in, chars, mean_in, tastes, coef_in, inv_in,
    out, pairs, mk, home,
    fm, cols, mean, coef, inv,
    CA, TA, CF, TB, KEY, BT, sid, asked,
    IDC, RT, UP, X, XM, R, RM, XC, XCM, RC, RCM, CP, CC,
    UA, MS, PK, FV, WT,
    UB, SCB, SH, DG, PO, PX, PR, YS, YR, ST, SV, HV,
    i_s, a_s, a_r, x_s, x_r, f_s, f_r, g_s, g_r, m_s, m_r, c_s, c_r, k_s, k_r, cc_s, cc_r,
    ms_s, ms_r, px_s, px_r, y_s, y_r, o_s, o_r, st_s, st_r, h_s, h_r,
):
    me = lax.axis_index("prod")
    cons = lax.axis_index("cons")
    core = lax.rem(cons, 2)
    partner = cons + 1 - 2 * core
    across = lax.rem(cons + 2, 4)
    LP, K = chars.shape
    LI = tastes.shape[0]
    W = cols.shape[1]
    half = W // 2
    block = inv.shape[1]
    pp = LP // n
    nb, pb = LP // 128, pad // 128
    nc, nw, nt = LI // IC, LI // WC, LP // JT
    base = me * LP

    barrier = pltpu.get_barrier_semaphore()
    for d in range(1, n):
        pl.semaphore_signal(barrier, inc=1, device_id={"prod": lax.rem(me + d, n)}, device_id_type=MESH)
    for d in range(1, 4):
        pl.semaphore_signal(barrier, inc=1, device_id={"cons": lax.rem(cons + d, 4)}, device_id_type=MESH)

    def loop(fn, lo=1):
        def step(d, carry):
            fn(d)
            return carry
        lax.fori_loop(lo, n, step, 0)

    def to_prod(src, dst, s, r, d):
        return pltpu.make_async_remote_copy(
            src, dst, s, r,
            device_id={"prod": lax.rem(me + d, n)}, device_id_type=MESH,
        )

    rest = pl.ds(0, n - 1)

    def all_of(ref, s, r):
        return to_prod(ref, ref, s, r, 1)

    def to_cons(src, dst, s, r, peer):
        return pltpu.make_async_remote_copy(src, dst, s, r, device_id={"cons": peer}, device_id_type=MESH)

    small = [
        pltpu.make_async_copy(src, dst, i_s.at[2 + k])
        for k, (src, dst) in enumerate(((fm_in, fm), (mean_in, mean), (cols_in, cols), (coef_in, coef)))
    ]
    for copy in small:
        copy.start()
    load_chars = pltpu.make_async_copy(chars, CA.at[:, pl.ds(0, K)], i_s.at[0])
    load_tastes = pltpu.make_async_copy(tastes, TA.at[:, pl.ds(0, K)], i_s.at[1])
    load_chars.start()
    load_tastes.start()
    load_inv = pltpu.make_async_copy(inv_in, inv, i_s.at[6])
    load_inv.start()

    TA[:, K:] = jnp.where(lax.broadcasted_iota(jnp.int32, (LI, K), 1) < 3, 1.0, 0.0).astype(BF16)
    at0 = lax.broadcasted_iota(jnp.int32, (128, 128), 0)
    at1 = lax.broadcasted_iota(jnp.int32, (128, 128), 1)
    before = jnp.where(at0 < at1, 1.0, 0.0).astype(BF16)
    q0 = lax.broadcasted_iota(jnp.int32, (nb * n, nb * n), 0).astype(F32)
    q1 = lax.broadcasted_iota(jnp.int32, (nb * n, nb * n), 1).astype(F32)
    b0, b1 = jnp.floor((q0 + 0.5) * (1.0 / n)), jnp.floor((q1 + 0.5) * (1.0 / n))
    earlier = jnp.where((q0 - b0 * n == q1 - b1 * n) & (b1 < b0), 1.0, 0.0).astype(BF16)
    small[0].wait()
    fmf = fm[...].astype(F32)
    source = jnp.floor((fmf + 0.5) * (1.0 / LP))
    local = fmf - source * float(LP)
    owners = rows_of((n, 128))
    marks = jnp.concatenate(
        [jnp.where(source[:, b * 128:(b + 1) * 128] == owners, 1.0, 0.0) for b in range(nb)], axis=0
    )
    inner = jnp.dot(marks.astype(BF16), before, preferred_element_type=F32)
    totals = jnp.dot(marks.astype(BF16), jnp.ones((128, 128), BF16), preferred_element_type=F32)
    offset = jnp.dot(earlier, totals.astype(BF16), preferred_element_type=F32)
    placed = marks * (inner + offset)
    slot = jnp.concatenate(
        [jnp.sum(placed[b * n:(b + 1) * n], axis=0, keepdims=True) for b in range(nb)], axis=1
    )
    high = jnp.floor((slot + 0.5) * (1.0 / 128))
    KEY[...] = source * float(pb) + high
    BT[...] = jnp.where(slot - high * 128.0 == rows_of((128, LP)), 1.0, 0.0).astype(BF16)

    def scatter(parts):
        mask = KEY[...] == rows_of((n * pb, LP))
        left = jnp.concatenate([jnp.where(mask, p, 0.0) for p in parts], axis=0).astype(BF16)
        got = lax.dot_general(left, BT[...], NT, preferred_element_type=F32)
        return [got[k * n * pb:(k + 1) * n * pb] for k in range(len(parts))]

    upper = jnp.floor((local + 0.5) * (1.0 / 128))
    hi, lo = scatter([upper, local - upper * 128.0])
    q = rows_of((n * pb, 128))
    owner = jnp.floor((q + 0.5) * (1.0 / pb))
    place = (q - owner * pb) * 128.0 + lax.broadcasted_iota(jnp.int32, (n * pb, 128), 1).astype(F32)
    wanted = jnp.where(place < float(pp), owner * float(LP) + hi * 128.0 + lo, -1.0).astype(jnp.int32)
    for p in range(n):
        for b in range(pb):
            sid[p, :, b * 128:(b + 1) * 128] = wanted[p * pb + b:p * pb + b + 1]

    small[1].wait()
    for g in range(nb):
        CA[g * 128:(g + 1) * 128, K:] = split(turned(mean[:, g * 128:(g + 1) * 128]), K)
    pl.semaphore_wait(barrier, n + 2)

    def a_copy(d):
        return to_prod(sid.at[lax.rem(me + d, n)], asked.at[me], a_s.at[0], a_r.at[d], d)

    loop(lambda d: a_copy(d).start())
    asked[me] = sid[me]

    small[2].wait()
    small[3].wait()
    load_chars.wait()

    def pick(wants):
        spot = lax.broadcasted_iota(jnp.int32, (128, 128), 1).astype(F32)
        bands = []
        for w in wants:
            want = turned((w - base).astype(F32))
            bands.append(jnp.concatenate(
                [jnp.where(want == spot + float(b * 128), 1.0, 0.0).astype(BF16) for b in range(nb)], axis=1
            ))
        got = jnp.dot(jnp.concatenate(bands, axis=0), CA[...], preferred_element_type=F32)
        means = []
        for k in range(len(wants)):
            t = got[k * 128:(k + 1) * 128, K:].T
            means.append(t[0:1] + (t[1:2] + t[2:3]))
        return got[:, :K].astype(BF16), means

    rows, means = pick([cols[:, g * 128:(g + 1) * 128] for g in range(W // 128)])
    XC[:, :cp, :] = rows.astype(F32).reshape(n, cp, K).astype(BF16)
    for g in range(W // 128):
        XCM[:, g * 128:(g + 1) * 128] = means[g]

    def c_copy(d):
        return to_prod(XC.at[lax.rem(me + d, n)], RC.at[me], c_s.at[0], c_r.at[0], d)

    def k_copy(d):
        return to_prod(XCM, RCM.at[me], k_s.at[0], k_r.at[0], d)

    loop(lambda d: c_copy(d).start())
    loop(lambda d: k_copy(d).start())
    RC[me] = XC[me]
    RCM[me] = XCM[...]

    def ms_copy(d, ic):
        return to_prod(MS.at[0, ic], MS.at[d, ic], ms_s.at[ic], ms_r.at[ic], d)

    def stats(ic, carry):
        i0 = pl.multiple_of(ic * IC, IC)
        u = lax.dot_general(CA[...], TA[pl.ds(i0, IC), :], NT, preferred_element_type=F32)
        UA[...] = u
        m = jnp.maximum(jnp.max(u, axis=0, keepdims=True), 0.0)
        s8 = jnp.sum(jnp.exp(UA[...] - m).reshape(LP // 8, 8, IC), axis=0)
        MS[0, ic, 0:1, :] = m
        MS[0, ic, 1:2, :] = jnp.sum(s8, axis=0, keepdims=True)
        loop(lambda d: ms_copy(d, ic).start())
        return carry

    def cc_copy(d):
        return to_prod(CP, CC.at[me], cc_s.at[0], cc_r.at[0], d)

    span = pad // 4

    def quarter(c):
        return pl.ds(pl.multiple_of(c * span, span), span)

    part, other = quarter(cons), quarter(across)

    def x_copy(d):
        return to_prod(X.at[lax.rem(me + d, n)], R.at[me, part], x_s.at[0], x_r.at[d], d)

    def m_copy(d):
        return to_prod(XM.at[lax.rem(me + d, n)], RM.at[me], m_s.at[0], m_r.at[0], d)

    def g_copy(d, batch):
        src = lax.rem(me + n - d, n)
        return to_cons(R.at[src, part], R.at[src, part], g_s.at[0], g_r.at[batch], across)

    def f_copy(d, which):
        src = lax.rem(me + n - d, n)
        return to_cons(R.at[src, which], R.at[src, which], f_s.at[0], f_r.at[0], partner)

    load_tastes.wait()
    lax.fori_loop(0, 1, stats, 0)
    loop(lambda d: a_copy(d).wait_recv())
    for p in range(n):
        for b in range(pb):
            IDC[p, b * 128:(b + 1) * 128, :] = turned((asked[p, :, b * 128:(b + 1) * 128] - base).astype(F32))
    spot = lax.broadcasted_iota(jnp.int32, (1, 128), 1).astype(F32)

    def hots(want):
        return jnp.concatenate(
            [jnp.where(want == spot + float(b * 128), 1.0, 0.0).astype(BF16) for b in range(nb)], axis=1
        )

    asks = jnp.concatenate([hots(IDC[p, part, :]) for p in range(n)], axis=0)
    got = jnp.dot(asks, CA[:, :K], preferred_element_type=F32).astype(BF16)
    for p in range(n):
        X[p] = got[p * span:(p + 1) * span]
    loop(lambda d: x_copy(d).start())
    idf = (jnp.concatenate([asked[p] for p in range(n)], axis=1) - base).astype(F32)
    up = jnp.floor((idf + 0.5) * (1.0 / 128))
    RT[...] = jnp.where(idf - up * 128.0 == rows_of((128, n * pad)), 1.0, 0.0).astype(BF16)
    UP[...] = up
    grid = jnp.concatenate([mean[:, b * 128:(b + 1) * 128] for b in range(nb)], axis=0)
    found = jnp.dot(jnp.concatenate(thirds(grid), axis=0).astype(BF16), RT[...], preferred_element_type=F32)
    found = found[:nb] + (found[nb:2 * nb] + found[2 * nb:])
    means = jnp.sum(jnp.where(up == rows_of((nb, n * pad)), found, 0.0), axis=0, keepdims=True)
    for p in range(n):
        XM[p] = means[:, p * pad:(p + 1) * pad]
    loop(lambda d: m_copy(d).start())
    all_of(sid.at[rest], a_s.at[0], a_r.at[0]).wait_send()
    all_of(RC.at[rest], c_s.at[0], c_r.at[0]).wait()
    all_of(RCM.at[rest], k_s.at[0], k_r.at[0]).wait()
    total = RC[0, :cp, :].astype(F32)
    heads = RCM[0]
    for p in range(1, n):
        total = total + RC[p, :cp, :].astype(F32)
        heads = heads + RCM[p]
    CP[:cp, :] = total.astype(BF16)
    loop(lambda d: cc_copy(d).start())
    CC[me] = CP[...]
    R[me] = jnp.dot(hots(IDC[me]), CA[:, :K], preferred_element_type=F32).astype(BF16)

    RM[me] = XM[me]
    held = max(nc - 1, 1)
    lax.fori_loop(1, held, stats, 0)

    first = n // 2

    def pass_on(batch, lo, hi):
        def step(d, carry):
            x_copy(d).wait_recv()
            f_copy(d, part).start()
            return carry
        lax.fori_loop(lo, hi, step, 0)
        def across_step(d, carry):
            g_copy(d, batch).start()
            return carry
        lax.fori_loop(lo, hi, across_step, 0)

    def hand_over(batch, lo, hi):
        all_of(R.at[pl.ds(0, hi - lo), part], g_s.at[0], g_r.at[batch]).wait_recv()
        def step(d, carry):
            f_copy(d, other).start()
            return carry
        lax.fori_loop(lo, hi, step, 0)

    pass_on(0, 1, first)
    pass_on(1, first, n)
    lax.fori_loop(held, nc, stats, 0)
    hand_over(0, 1, first)

    all_of(CC.at[rest], cc_s.at[0], cc_r.at[0]).wait()
    ccv = CC[:, :cp, :].astype(F32).reshape(n * cp, K).astype(BF16)
    cm = jnp.concatenate([turned(heads[:, g * 128:(g + 1) * 128])[:, :1] for g in range(W // 128)], axis=0)

    def weights(ic):
        all_of(MS.at[pl.ds(1, n - 1), ic], ms_s.at[ic], ms_r.at[ic]).wait()
        for w in range(IC // WC):
            i0 = pl.multiple_of(ic * IC + w * WC, WC)
            at = slice(w * WC, (w + 1) * WC)
            peak = MS[0, ic, 0:1, at]
            for d in range(1, n):
                peak = jnp.maximum(peak, MS[d, ic, 0:1, at])
            den = jnp.exp(-peak)
            for d in range(n):
                den = den + MS[d, ic, 1:2, at] * jnp.exp(MS[d, ic, 0:1, at] - peak)
            f = count_products / den
            PK[:, pl.ds(i0, WC)] = peak
            FV[:, pl.ds(i0, WC)] = f
            cu = lax.dot_general(ccv, TA[pl.ds(i0, WC), :K], NT, preferred_element_type=F32) + cm
            w = coef[:, pl.ds(i0, WC)] * (f * jnp.exp(cu - peak))
            WT[pl.ds(i0, WC), :] = w.astype(BF16).T

    def weights_step(ic, carry):
        weights(ic)
        return carry

    lax.fori_loop(0, min(1, held), weights_step, 0)
    hand_over(1, first, n)
    lax.fori_loop(min(1, held), held, weights_step, 0)
    all_of(R.at[rest, part], g_s.at[0], g_r.at[0]).wait_send()
    all_of(X.at[rest], x_s.at[0], x_r.at[0]).wait_send()

    all_of(RM.at[rest], m_s.at[0], m_r.at[0]).wait()
    for p in range(n):
        for b in range(pb):
            at = p * pad + b * 128
            TB[at:at + 128, K:] = split(turned(RM[p, :, b * 128:(b + 1) * 128]), K)
    all_of(R.at[rest, pl.ds(0, 2 * span)], f_s.at[0], f_r.at[0]).wait()

    for p in range(n):
        TB[p * pad:(p + 1) * pad, :K] = R[p]

    def firm(g, carry):
        bands = []
        for h in range(8):
            rows = pl.ds(pl.multiple_of(g * 1024 + h * 128, 128), 128)
            want = turned(fm[:, rows].astype(F32))
            bands.append(jnp.concatenate(
                [
                    jnp.where(want == sid[p, :, b * 128:(b + 1) * 128].astype(F32), 1.0, 0.0).astype(BF16)
                    for p in range(n) for b in range(pb)
                ],
                axis=1,
            ))
        rows = pl.ds(pl.multiple_of(g * 1024, 1024), 1024)
        CF[rows, :] = jnp.dot(jnp.concatenate(bands, axis=0), TB[...], preferred_element_type=F32).astype(BF16)
        return carry

    lax.fori_loop(0, LP // 1024, firm, 0)

    lax.fori_loop(held, nc, weights_step, 0)


    def tile_rows(jt):
        return pl.ds(pl.multiple_of(jt * JT, JT), JT)

    def px_copy(jt):
        rows = tile_rows(jt)
        return to_cons(PX.at[rows], PR.at[rows], px_s.at[0], px_r.at[jt], partner)

    def y_copy(jt):
        rows = tile_rows(jt)
        return to_cons(YS.at[rows], YR.at[rows], y_s.at[0], y_r.at[jt], across)

    mine = [pl.ds(pl.multiple_of(core * half + k * W, half), half) for k in range(2)]

    def o_copy(jt, k):
        rows = tile_rows(jt)
        return to_cons(out.at[rows, mine[k]], out.at[rows, mine[k]], o_s.at[0], o_r.at[0], partner)

    def st_copy(d, jt):
        rows = tile_rows(jt)
        return to_cons(
            ST.at[cons, :, rows], ST.at[cons, :, rows], st_s.at[0], st_r.at[0], lax.rem(cons + d, 4)
        )

    def forward(jt):
        rows = tile_rows(jt)
        px_copy(jt).wait_recv()
        YS[rows, :] = (PO[rows, :] + PR[rows, :]).astype(BF16)
        y_copy(jt).start()

    def finish(jt):
        y_copy(jt).wait_recv()
        rows = tile_rows(jt)
        x = (YS[rows, :].astype(F32) + YR[rows, :].astype(F32)) / count_consumers
        h = x.astype(BF16)
        out[rows, mine[0]] = h
        out[rows, mine[1]] = (x - h.astype(F32)).astype(BF16)
        o_copy(jt, 0).start()
        o_copy(jt, 1).start()

    heads_row = cols[...].astype(F32)

    def panel(jt, carry):
        rows = tile_rows(jt)
        UB[...] = lax.dot_general(CF[rows, :], TA[...], NT, preferred_element_type=F32)
        for g in range(JT // GR):
            band = pl.ds(g * GR, GR)
            sh = jnp.zeros((GR, 128), F32)
            dg = jnp.zeros((GR, 128), F32)
            for b in range(LI // 128):
                at = pl.ds(b * 128, 128)
                sc = jnp.exp(UB[band, at] - PK[:, at]) * FV[:, at]
                SCB[band, at] = sc.astype(BF16)
                sh = sh + sc
                dg = dg + sc * coef[:, at]
            SH[band, :] = sh
            DG[band, :] = dg
        acc = jnp.dot(SCB[...], WT[...], preferred_element_type=F32)
        ST[cons, 0:1, rows] = jnp.sum(SH[...].T, axis=0, keepdims=True)
        diag = jnp.sum(DG[...], axis=1, keepdims=True)
        ids = jnp.concatenate(
            [
                turned(fm[:, pl.ds(pl.multiple_of(jt * JT + b * 128, 128), 128)].astype(F32))[:, :1]
                for b in range(JT // 128)
            ],
            axis=0,
        )
        acc = acc - jnp.where(ids == heads_row, diag, 0.0)
        first, second = acc[:, :half], acc[:, half:]
        PO[rows, :] = jnp.where(core == 0, first, second)
        PX[rows, :] = jnp.where(core == 0, second, first)
        px_copy(jt).start()
        for d in range(1, 4):
            st_copy(d, jt).start()

        @pl.when(jt > 0)
        def _():
            forward(jt - 1)

        @pl.when(jt > 3)
        def _():
            finish(jt - 4)

        return carry

    lax.fori_loop(0, nt, panel, 0)
    forward(nt - 1)
    all_of(ST.at[pl.ds(0, 3)], st_s.at[0], st_r.at[0]).wait()
    share = (ST[0] + ST[1] + ST[2] + ST[3]) / count_consumers
    sums = scatter(thirds(share))
    slots = sums[0] + (sums[1] + sums[2])
    for p in range(n):
        for b in range(pb):
            SV[p, :, b * 128:(b + 1) * 128] = slots[p * pb + b:p * pb + b + 1]

    def h_copy(d):
        return to_prod(SV.at[lax.rem(me + d, n)], HV.at[me], h_s.at[0], h_r.at[0], d)

    loop(lambda d: h_copy(d).start())
    HV[me] = SV[me]
    load_inv.wait()
    s1 = share.astype(BF16).astype(F32)
    s2 = share - s1
    for b in range(inv.shape[0]):
        m = inv[b]
        mh = m.astype(BF16)
        pair = jnp.concatenate([mh, (m - mh.astype(F32)).astype(BF16)], axis=1)
        pairs[b] = pair
        at = slice(b * block, (b + 1) * block)
        left = jnp.concatenate(
            [jnp.broadcast_to(s1[:, at], (8, block)), jnp.broadcast_to(s2[:, at], (8, block))], axis=0
        ).astype(BF16)
        g = lax.dot_general(jnp.concatenate([left, left], axis=1), pair, NT, preferred_element_type=F32)
        mk[b:b + 1, :] = g[0:1] + g[8:9]
    for t in range(max(nt - 4, 0), nt):
        finish(t)
    all_of(HV.at[rest], h_s.at[0], h_r.at[0]).wait()
    back = jnp.concatenate([HV[p] for p in range(n)], axis=1)
    mask = UP[...] == rows_of((nb, n * pad))
    left = jnp.concatenate([jnp.where(mask, p, 0.0) for p in thirds(back)], axis=0).astype(BF16)
    got = lax.dot_general(left, RT[...], NT, preferred_element_type=F32)
    home[...] = got[:nb] + (got[nb:2 * nb] + got[2 * nb:])
    to_cons(PX, PR, px_s.at[0], px_r.at[0], partner).wait_send()
    to_cons(YS, YR, y_s.at[0], y_r.at[0], across).wait_send()
    to_cons(out.at[:, pl.ds(0, W)], out.at[:, pl.ds(0, W)], o_s.at[0], o_r.at[0], partner).wait()


def run(n, count_products, count_consumers, fm, cols, chars, mean, tastes, coef, inv):
    LP, K = chars.shape
    LI, W = tastes.shape[0], cols.shape[1]
    half = W // 2
    cp = W // n
    room = -(-cp // 16) * 16
    pad = lanes(LP // n)
    IC, WC, JT, GR = min(1024, LI), min(512, LI), min(256, LP), 32
    nc, nt = LI // IC, LP // JT
    nb, pb = LP // 128, pad // 128
    count, block = inv.shape[0], inv.shape[1]
    dma = pltpu.SemaphoreType.DMA
    vm = pltpu.VMEM
    I32 = jnp.int32
    ANY = pl.BlockSpec(memory_space=pltpu.HBM)
    return pl.pallas_call(
        functools.partial(
            step_kernel, n, cp, room, pad, float(count_products), float(count_consumers), IC, WC, JT, GR
        ),
        out_shape=(
            jax.ShapeDtypeStruct((LP, 2 * W), BF16),
            jax.ShapeDtypeStruct((count, block, 2 * block), BF16),
            jax.ShapeDtypeStruct((count, block), F32),
            jax.ShapeDtypeStruct((nb, 128), F32),
        ),
        in_specs=[ANY] * 7,
        out_specs=(VMEM,) * 4,
        scratch_shapes=[
            vm((1, LP), I32), vm((1, W), I32), vm((1, LP), F32), vm((1, LI), F32), vm(inv.shape, F32),
            vm((LP, 2 * K), BF16), vm((LI, 2 * K), BF16), vm((LP, 2 * K), BF16), vm((n * pad, 2 * K), BF16),
            vm((1, LP), F32), vm((128, LP), BF16),
            vm((n, 1, pad), I32), vm((n, 1, pad), I32),
            vm((n, pad, 128), F32), vm((128, n * pad), BF16), vm((1, n * pad), F32),
            vm((n, pad // 4, K), BF16), vm((n, 1, pad), F32), vm((n, pad, K), BF16), vm((n, 1, pad), F32),
            vm((n, room, K), BF16), vm((1, W), F32), vm((n, room, K), BF16), vm((n, 1, W), F32),
            vm((room, K), BF16), vm((n, room, K), BF16),
            vm((LP, IC), F32), vm((n, nc, 2, IC), F32), vm((1, LI), F32), vm((1, LI), F32), vm((LI, W), BF16),
            vm((JT, LI), F32), vm((JT, LI), BF16), vm((JT, 128), F32), vm((JT, 128), F32),
            vm((LP, half), F32), vm((LP, half), F32), vm((LP, half), F32),
            vm((LP, half), BF16), vm((LP, half), BF16),
            vm((4, 1, LP), F32), vm((n, 1, pad), F32), vm((n, 1, pad), F32),
        ] + [dma((7,)), dma((1,)), dma((n,)), dma((1,)), dma((n,))] + [dma((1,))] * 3 + [dma((2,))] + [dma((1,))] * 8
        + [dma((nc,))] * 2 + [dma((1,)), dma((nt,))] * 2 + [dma((1,))] * 6,
        compiler_params=pltpu.CompilerParams(collective_id=1, has_side_effects=True, vmem_limit_bytes=LIMIT),
    )(*[pltpu.with_memory_space_constraint(v, pltpu.HBM) for v in (fm, cols, chars, mean, tastes, coef, inv)])


def firm_kernel(x, pairs, mk, home, out, markup, shares):
    block = pairs.shape[1]
    W = out.shape[1]

    @pl.when(pl.program_id(0) == 0)
    def _():
        shares[...] = home[...]
        markup[...] = mk[...]

    per = out.shape[0] // block
    for b in range(per):
        rows = slice(b * block, (b + 1) * block)
        at = pl.program_id(0) * per + b
        both = x[pl.ds(pl.multiple_of(at * block, block), block), :]
        r = jnp.dot(pairs[at], jnp.concatenate([both, both], axis=0), preferred_element_type=F32)
        out[rows, :] = r[:, :W] + r[:, W:]


def firms(x, pairs, mk, home):
    LP, W = x.shape[0], x.shape[1] // 2
    count, block = pairs.shape[0], pairs.shape[1]
    per = min(8, count)
    whole = lambda a: pl.BlockSpec(a.shape, lambda i: (0, 0))
    return pl.pallas_call(
        firm_kernel,
        grid=(count // per,),
        out_shape=(
            jax.ShapeDtypeStruct((LP, W), F32),
            jax.ShapeDtypeStruct(mk.shape, F32),
            jax.ShapeDtypeStruct(home.shape, F32),
        ),
        in_specs=[
            VMEM,
            VMEM,
            whole(mk),
            whole(home),
        ],
        out_specs=(pl.BlockSpec((per * block, W), lambda i: (i, 0)), whole(mk), whole(home)),
        compiler_params=pltpu.CompilerParams(vmem_limit_bytes=16 * 1024 * 1024),
    )(x, pairs, mk, home)


def body(tastes, price_coef, characteristics, mean_utility, panel_cols, firm_map, inverses):
    n = lax.axis_size("prod")
    LP = characteristics.shape[0]
    jacobian, pairs, mk, home = run(
        n, LP * n, tastes.shape[0] * lax.axis_size("cons"),
        firm_map[None, :], panel_cols[None, :], characteristics, mean_utility[None, :],
        tastes, price_coef[None, :], inverses,
    )
    response, markup, shares = firms(jacobian, pairs, mk, home)
    return shares.reshape(LP), markup.reshape(LP), response


def solution(mesh):
    return jax.shard_map(
        body,
        mesh=mesh,
        in_specs=(
            P("cons", None),
            P("cons"),
            P("prod", None),
            P("prod"),
            P(),
            P("prod"),
            P("prod", None, None),
        ),
        out_specs=(P("prod"), P("prod"), P("prod", None)),
        check_vma=False,
    )
```
